1024 devices in a mesh: gx: 32 (over z), gy: 4 (over x_lo, core), gz: 8 (over x_hi, y).
Axes of the slice: x: 4 (x_hi: 2, x_lo: 2; x = x_hi * 2 + x_lo), y: 4, z: 32, core: 2. Of those that a mesh axis runs over, the one named last changes fastest.
Arguments:
- orbitals: float32 [32, 4, 8, 96, 4096], P('gx', 'gy', 'gz'), may hold values from -6 to 6
- potential: float32 [256, 32, 64], P('gx', 'gy', 'gz'), may hold values from -1.5 to 1.5
- coefficients: float32 [32, 4, 8, 96, 256], P('gx', 'gy', 'gz'), may hold values from -0.6 to 0.6
Outputs:
- filtered_coefficients: float32 [32, 4, 8, 96, 256], P('gx', 'gy', 'gz')
The draws below stay inside these ranges and needn't reach their ends.
All inputs are finite; a program needn't handle non-finite values.
Results may differ from the reference program's by a relative error of at most 0.0003.
Values sent between devices are 32-bit elements; how exact they have to be, the bound alone decides.
No kernel may reach another device: no remote copies, remote signals or barrier semaphores. Data moves between devices by JAX's collectives and lax.ppermute only.
A program may use at most 32 MiB of HBM per device.

```python
import jax
import jax.numpy as jnp
from jax import lax

ORBITAL_TOTAL = 96
COEFFICIENT_COLS = 256
EDGE = 8
CHEB = 2
NEWTON = 6
DG_STEPS = 3
ELEMENTS_FIRST = 32
ELEMENTS_SECOND = 4
ELEMENTS_THIRD = 8
NXC = 256
NYC = 32
NZC = 64
EXTENDED_CELLS = 4096


def levels(stream_key, extent, shards, low, largest):
    gain, own = 1.0, jax.random.fold_in(stream_key, 6)
    for axis_at, parts in shards:
        heights = jnp.exp(jax.random.uniform(jax.random.fold_in(own, axis_at), (parts,), jnp.float32, low / len(shards), largest / len(shards)))
        gain = gain * jnp.repeat(heights, extent[axis_at] // parts).reshape([-1 if axis == axis_at else 1 for axis in range(len(extent))])
    return gain


def noise(rng, shape, width, reach, pieces=(), held_as=jnp.bfloat16):
    drawn = width * jax.random.normal(rng, shape, jnp.float32)
    if pieces:
        drawn = drawn * levels(rng, shape, pieces, -0.22, 0.18)
    return jnp.clip(drawn, -reach, reach).astype(held_as)


def setup_inputs(seed: int = 0) -> dict:
    splits = jax.random.split(jax.random.key(seed), 4)
    orbitals = noise(splits[0], (ELEMENTS_FIRST, ELEMENTS_SECOND, ELEMENTS_THIRD, ORBITAL_TOTAL, EXTENDED_CELLS), 1.0, 6.0, ((0, 32), (1, 4), (2, 8)), jnp.float32)
    potential = jnp.clip(jax.random.uniform(splits[1], (NXC, NYC, NZC), jnp.float32, -1.5, 1.5) * levels(splits[1], (NXC, NYC, NZC), ((0, 32), (1, 4), (2, 8)), -0.4, 0.0), -1.5, 1.5)
    coefficients = noise(splits[2], (ELEMENTS_FIRST, ELEMENTS_SECOND, ELEMENTS_THIRD, ORBITAL_TOTAL, COEFFICIENT_COLS), 0.1, 0.6, ((0, 32), (1, 4), (2, 8)), jnp.float32)
    return dict(orbitals=orbitals, potential=potential, coefficients=coefficients)


cutoff = 1.0

def matmul(left, right):
    return jnp.dot(left, right, precision=lax.Precision.HIGHEST, preferred_element_type=jnp.float32)

def box_masks(length):
    position = jnp.arange(length ** 3, dtype=jnp.int32)
    coordinates = (position // (length * length), position // length % length, position % length)
    mask_list = []
    for coordinate, stride in zip(coordinates, (length * length, length, 1)):
        mask_list.append((stride, (coordinate > 0).astype(jnp.float32), (coordinate < length - 1).astype(jnp.float32)))
    return mask_list

def apply_box(vectors, potential_flat, length):
    area = length * length
    cells = length ** 3
    padded = jnp.pad(vectors, ((0, 0), (area, area)))
    total = jnp.zeros_like(vectors)
    for stride, lower_ok, upper_ok in box_masks(length):
        total = total + lower_ok * padded[:, area - stride:area - stride + cells] + upper_ok * padded[:, area + stride:area + stride + cells]
    return (3.0 + potential_flat) * vectors - 0.5 * total

def chebyshev(operator, initial, degree, centre, half_width):
    prior_vectors = initial
    current = (operator(initial) - centre * initial) / half_width
    for repeat in range(degree - 1):
        following = 2.0 * (operator(current) - centre * current) / half_width - prior_vectors
        prior_vectors, current = (current, following)
    return current

def inverse_root(intersection, newton_count):
    sigma = jnp.sqrt(jnp.sum(intersection * intersection))
    identity = jnp.eye(intersection.shape[0], dtype=jnp.float32)
    current = intersection / sigma
    inverse = identity
    for repeat in range(newton_count):
        factor = 1.5 * identity - 0.5 * matmul(inverse, current)
        current = matmul(current, factor)
        inverse = matmul(factor, inverse)
    return inverse / jnp.sqrt(sigma)

def element_basis(orbital_rows, ext_potential, length, centre, half_width):
    doubled = 2 * length
    potential_flat = ext_potential.reshape(doubled ** 3)

    def extended_operator(vectors):
        return apply_box(vectors, potential_flat, doubled)
    filtered = chebyshev(extended_operator, orbital_rows, CHEB, centre, half_width)
    lower = length // 2
    restricted = filtered.reshape(-1, doubled, doubled, doubled)[:, lower:lower + length, lower:lower + length, lower:lower + length]
    restricted = restricted.reshape(-1, length ** 3)
    intersection = matmul(restricted, restricted.T)
    basis = matmul(inverse_root(intersection, NEWTON), restricted)
    own_potential = ext_potential[lower:lower + length, lower:lower + length, lower:lower + length].reshape(length ** 3)
    diagonal_block = matmul(basis, apply_box(basis, own_potential, length).T)
    return (basis, diagonal_block)

def pair_block(own_face, other_face):
    return -0.5 * jnp.einsum('xyzac,xyzbc->xyzab', own_face, other_face, precision=lax.Precision.HIGHEST)

def reference(orbitals, potential, coefficients):
    length = EDGE
    grid_x, grid_y, grid_z = (orbitals.shape[0], orbitals.shape[1], orbitals.shape[2])
    spectrum_top = 6.0 + jnp.max(potential)
    centre = (spectrum_top + cutoff) / 2.0
    half_width = (spectrum_top - cutoff) / 2.0
    padded = jnp.pad(potential, ((length, 0), (length, 0), (length, 0)), mode='wrap')
    orbital_flat = orbitals.reshape(grid_x * grid_y * grid_z, orbitals.shape[3], orbitals.shape[4])

    def per_element(index):
        index_x = (index // (grid_y * grid_z)).astype(jnp.int32)
        index_y = (index // grid_z % grid_y).astype(jnp.int32)
        index_z = (index % grid_z).astype(jnp.int32)
        ext_potential = lax.dynamic_slice(padded, (index_x * length, index_y * length, index_z * length), (2 * length, 2 * length, 2 * length))
        return element_basis(orbital_flat[index], ext_potential, length, centre, half_width)
    bases, block_list = lax.map(per_element, jnp.arange(grid_x * grid_y * grid_z, dtype=jnp.int32))
    orbital_count = orbitals.shape[3]
    cube = bases.reshape(grid_x, grid_y, grid_z, orbital_count, length, length, length)
    block_list = block_list.reshape(grid_x, grid_y, grid_z, orbital_count, orbital_count)
    shape_face = (grid_x, grid_y, grid_z, orbital_count, length * length)
    low_x = cube[:, :, :, :, 0, :, :].reshape(shape_face)
    high_x = cube[:, :, :, :, length - 1, :, :].reshape(shape_face)
    low_y = cube[:, :, :, :, :, 0, :].reshape(shape_face)
    high_y = cube[:, :, :, :, :, length - 1, :].reshape(shape_face)
    low_z = cube[:, :, :, :, :, :, 0].reshape(shape_face)
    high_z = cube[:, :, :, :, :, :, length - 1].reshape(shape_face)
    couplings = ((pair_block(low_x, jnp.roll(high_x, 1, axis=0)), 1, 0), (pair_block(high_x, jnp.roll(low_x, -1, axis=0)), -1, 0), (pair_block(low_y, jnp.roll(high_y, 1, axis=1)), 1, 1), (pair_block(high_y, jnp.roll(low_y, -1, axis=1)), -1, 1), (pair_block(low_z, jnp.roll(high_z, 1, axis=2)), 1, 2), (pair_block(high_z, jnp.roll(low_z, -1, axis=2)), -1, 2))

    def galerkin(vectors):
        result = jnp.einsum('xyzab,xyzbc->xyzac', block_list, vectors, precision=lax.Precision.HIGHEST)
        for coupling, amount, axis_index in couplings:
            result = result + jnp.einsum('xyzab,xyzbc->xyzac', coupling, jnp.roll(vectors, amount, axis=axis_index), precision=lax.Precision.HIGHEST)
        return result
    return chebyshev(galerkin, coefficients, DG_STEPS, centre, half_width)
```

```python
import jax
import jax.numpy as jnp
from jax import lax
from jax.experimental import pallas as pl
from jax.experimental.pallas import tpu as pltpu
from jax.sharding import PartitionSpec as P

NEWTON = 6
DG_STEPS = 3
ROWS = 96
EDGE = 8
FLAT = EDGE * EDGE
COLS = 256
FACES = 6
BODY = FACES * FLAT
WIDTH = 512
cutoff = 1.0


def shifted(shard, axis, by):
    count = lax.axis_size(axis)
    return lax.ppermute(shard, axis, [(i, (i + by) % count) for i in range(count)])


def split(value):
    high = value.astype(jnp.bfloat16)
    low = (value - high.astype(jnp.float32)).astype(jnp.bfloat16)
    return high, low


def dot3(left, right, dims=(((1,), (0,)), ((), ()))):
    lh, ll = left
    rh, rl = right

    def one(a, b):
        return lax.dot_general(a, b, dims, preferred_element_type=jnp.float32)

    return one(lh, rh) + (one(lh, rl) + one(ll, rh))


def exact(left, right, dims=(((1,), (0,)), ((), ()))):
    return lax.dot_general(
        left, right, dims, precision=lax.Precision.HIGHEST, preferred_element_type=jnp.float32
    )


def lane_roll(value, by):
    return pltpu.roll(value, by % value.shape[-1], axis=value.ndim - 1)


def lanes(shape):
    return lax.broadcasted_iota(jnp.int32, shape, len(shape) - 1)


def basis_kernel(tiles_ref, orbitals_ref, vectors_ref, df_ref, ft_ref, scal_ref, traces_ref,
                 w_ref, restricted_ref, bt_ref):
    gy = lax.axis_index("gy")
    gz = lax.axis_index("gz")
    ny = lax.axis_size("gy")
    nz = lax.axis_size("gz")
    py = lax.rem(gy + ny - 1, ny)
    pz = lax.rem(gz + nz - 1, nz)
    near = lanes((8, 128)) % 16 < 8
    tallest = jnp.max(jnp.max(tiles_ref[...], axis=0)[5:6])
    top = 6.0 + tallest
    centre = (top + cutoff) / 2.0
    half_width = (top - cutoff) / 2.0
    scal_ref[0] = centre
    scal_ref[1] = half_width
    own_x, prior_x = [], []
    for row in (py, gy):
        low = tiles_ref[row * nz + pz]
        high = tiles_ref[row * nz + gz]
        own_x.append(jnp.where(near, low, lane_roll(high, 8)))
        prior_x.append(jnp.where(near, lane_roll(low, -8), high))
    own_x = jnp.concatenate(own_x, axis=1)
    prior_x = jnp.concatenate(prior_x, axis=1)
    planes = {}
    for plane in range(3, 13):
        source, row = (prior_x, plane) if plane < 8 else (own_x, plane - 8)
        planes[plane] = jnp.broadcast_to(source[row : row + 1], (8, 256))
        w_ref[plane - 3] = planes[plane] + (3.0 - centre)
    first_half = lanes((8, 128)) % 16 < 8

    def packed(even, odd):
        return jnp.where(first_half, lane_roll(even, -68)[:, :128], lane_roll(odd, -60)[:, :128])

    inverse = 1.0 / half_width

    def around(value):
        return (
            lane_roll(value, 1) + lane_roll(value, -1) + lane_roll(value, 16) + lane_roll(value, -16)
        )

    def filter_rows(step, carry):
        rows = pl.ds(pl.multiple_of(step * 8, 8), 8)
        start = {p: orbitals_ref[rows, p * 256 : (p + 1) * 256] for p in range(2, 14)}
        once = {}
        for p in range(3, 13):
            total = around(start[p]) + (start[p - 1] + start[p + 1])
            once[p] = (w_ref[p - 3] * start[p] - 0.5 * total) * inverse
        twice = {}
        for p in range(4, 12):
            total = around(once[p]) + (once[p - 1] + once[p + 1])
            twice[p] = (w_ref[p - 3] * once[p] - 0.5 * total) * (2.0 * inverse) - start[p]
        for q in range(4):
            restricted_ref[rows, q * 128 : (q + 1) * 128] = packed(twice[4 + 2 * q], twice[5 + 2 * q])
        return carry

    lax.fori_loop(0, ROWS // 8, filter_rows, 0)
    restricted = restricted_ref[...]
    halves = split(restricted)
    intersection = exact(restricted, restricted, (((1,), (1,)), ((), ())))
    sigma = jnp.sqrt(jnp.sum(intersection * intersection))
    identity = (
        lax.broadcasted_iota(jnp.int32, (ROWS, ROWS), 0) == lanes((ROWS, ROWS))
    ).astype(jnp.float32)
    current = intersection / sigma
    factor = 1.5 * identity - 0.5 * current
    current = exact(current, factor)
    root = factor
    for _ in range(NEWTON - 1):
        factor = 1.5 * identity - 0.5 * exact(root, current)
        current = exact(current, factor)
        root = exact(factor, root)
    root = root / jnp.sqrt(sigma)
    basis = dot3(split(root), halves)

    own = jnp.concatenate([packed(planes[4 + 2 * q], planes[5 + 2 * q]) for q in range(4)], axis=1)
    own = own[:1] + 3.0
    cell = lanes((ROWS, WIDTH))
    z = cell % 8
    y = cell // 16 % 8
    x = cell // 128 * 2 + cell // 8 % 2
    odd = x % 2 == 1

    def gate(ok, value):
        return jnp.where(ok, value, 0.0)

    total = gate(z > 0, lane_roll(basis, 1)) + gate(z < 7, lane_roll(basis, -1))
    total = total + gate(y > 0, lane_roll(basis, 16)) + gate(y < 7, lane_roll(basis, -16))
    total = total + jnp.where(odd, lane_roll(basis, 8), lane_roll(basis, -8))
    total = total + gate(
        (x > 0) & (x < 7), jnp.where(odd, lane_roll(basis, -120), lane_roll(basis, 120))
    )
    applied = own * basis - 0.5 * total
    diagonal = dot3(split(basis), split(applied), (((1,), (1,)), ((), ())))

    bt_ref[...] = jnp.concatenate([basis, jnp.zeros((128 - ROWS, WIDTH), jnp.float32)], axis=0).T
    pieces = [
        jnp.concatenate([bt_ref[yy * 16 : yy * 16 + 8] for yy in range(8)], axis=0),
        jnp.concatenate([bt_ref[392 + yy * 16 : 400 + yy * 16] for yy in range(8)], axis=0),
        jnp.concatenate([bt_ref[q * 128 : q * 128 + 16] for q in range(4)], axis=0),
        jnp.concatenate([bt_ref[q * 128 + 112 : q * 128 + 128] for q in range(4)], axis=0),
        bt_ref[pl.ds(0, FLAT, stride=8)],
        bt_ref[pl.ds(7, FLAT, stride=8)],
    ]
    faces_t = jnp.concatenate(pieces, axis=0)
    ft_ref[...] = faces_t[:, :ROWS]
    df_ref[:, :BODY] = -0.5 * faces_t.T[:ROWS]
    df_ref[:, BODY : BODY + ROWS] = diagonal
    df_ref[:, BODY + ROWS :] = jnp.zeros((ROWS, WIDTH - BODY - ROWS), jnp.float32)
    traces = dot3(split(faces_t[:, :ROWS]), split(vectors_ref[...]))
    for face in range(FACES):
        traces_ref[face] = traces[face * FLAT : (face + 1) * FLAT]


def step_kernel(first, last, scal_ref, df_ref, ft_ref, now_ref, prior_ref, *refs):
    halo_refs, out_refs = refs[:FACES], refs[FACES:]
    now = now_ref[...]
    stacked = jnp.concatenate(
        [r[...] for r in halo_refs] + [now, jnp.zeros((WIDTH - BODY - ROWS, COLS), jnp.float32)], axis=0
    )
    result = dot3(split(df_ref[...]), split(stacked))
    centre, half_width = scal_ref[0], scal_ref[1]
    if first:
        following = (result - centre * now) / half_width
    else:
        following = 2.0 * (result - centre * now) / half_width - prior_ref[...]
    out_refs[0][...] = following
    if not last:
        traces = dot3(split(ft_ref[...]), split(following))
        for face in range(FACES):
            out_refs[1][face] = traces[face * FLAT : (face + 1) * FLAT]


def vmem():
    return pl.BlockSpec(memory_space=pltpu.VMEM)


def smem():
    return pl.BlockSpec(memory_space=pltpu.SMEM)


def per_device(orbitals, potential, coefficients):
    nx = lax.axis_size("gx")
    plane = lax.axis_size("gy") * lax.axis_size("gz")
    spread = jnp.pad(potential, ((0, 0), (0, 0), (0, 8))).reshape(8, 128)
    below = shifted(spread, "gx", 1)
    peak = jnp.broadcast_to(jnp.max(potential), (nx, 1, 128))
    peak = jnp.max(lax.all_to_all(peak, "gx", 0, 0))
    near = lanes((8, 128)) % 16 < 8
    row = lax.broadcasted_iota(jnp.int32, (8, 128), 0)
    block = jnp.where(near, jnp.where(row == 5, peak, spread), jnp.roll(below, 8, axis=1))
    tiles = lax.all_to_all(jnp.broadcast_to(block, (plane, 8, 128)), ("gy", "gz"), 0, 0)

    f32 = jnp.float32
    rows = orbitals.reshape(ROWS, -1)
    start = coefficients.reshape(ROWS, COLS)
    df, ft, scal, traces = pl.pallas_call(
        basis_kernel,
        out_shape=(
            jax.ShapeDtypeStruct((ROWS, WIDTH), f32),
            jax.ShapeDtypeStruct((BODY, ROWS), f32),
            jax.ShapeDtypeStruct((2,), f32),
            jax.ShapeDtypeStruct((FACES, FLAT, COLS), f32),
        ),
        in_specs=[vmem(), vmem(), vmem()],
        out_specs=(vmem(), vmem(), smem(), vmem()),
        scratch_shapes=[
            pltpu.VMEM((10, 8, 256), f32),
            pltpu.VMEM((ROWS, WIDTH), f32),
            pltpu.VMEM((WIDTH, 128), f32),
        ],
        name="basis",
    )(tiles, rows, start)

    prior, now = start, start
    for step in range(DG_STEPS):
        halos = []
        for at, axis in enumerate(("gx", "gy", "gz")):
            halos.append(shifted(traces[2 * at + 1], axis, 1))
            halos.append(shifted(traces[2 * at], axis, -1))
        last = step == DG_STEPS - 1
        shapes = [jax.ShapeDtypeStruct((ROWS, COLS), f32)]
        if not last:
            shapes.append(jax.ShapeDtypeStruct((FACES, FLAT, COLS), f32))

        def body(*refs, step=step, last=last):
            step_kernel(step == 0, last, *refs)

        results = pl.pallas_call(
            body,
            out_shape=tuple(shapes),
            in_specs=[smem()] + [vmem()] * (4 + FACES),
            out_specs=tuple(vmem() for _ in shapes),
            name=f"step{step}",
        )(scal, df, ft, now, prior, *halos)
        prior, now = now, results[0]
        if not last:
            traces = results[1]
    return now.reshape(coefficients.shape)


def solution(mesh):
    placed = (P("gx", "gy", "gz", None, None), P("gx", "gy", "gz"), P("gx", "gy", "gz", None, None))
    return jax.shard_map(
        per_device,
        mesh=mesh,
        in_specs=placed,
        out_specs=P("gx", "gy", "gz", None, None),
        check_vma=False,
    )
```

```python
import jax
import jax.numpy as jnp
from jax import lax
from jax.experimental import pallas as pl
from jax.experimental.pallas import tpu as pltpu
from jax.sharding import PartitionSpec as P

NEWTON = 6
DG_STEPS = 3
SHIFT = 3.0
ROWS = 96
EDGE = 8
FLAT = EDGE * EDGE
COLS = 256
FACES = 6
CUBE = 8
GRANT = 16 << 20
BODY = FACES * FLAT
WIDTH = 512
cutoff = 1.0


def shifted(shard, axis, by):
    count = lax.axis_size(axis)
    return lax.ppermute(shard, axis, [(i, (i + by) % count) for i in range(count)])


def split(value):
    high = value.astype(jnp.bfloat16)
    low = (value - high.astype(jnp.float32)).astype(jnp.bfloat16)
    return high, low


def dot3(left, right, dims=(((1,), (0,)), ((), ()))):
    lh, ll = left
    rh, rl = right

    def one(a, b):
        return lax.dot_general(a, b, dims, preferred_element_type=jnp.float32)

    return one(lh, rh) + (one(lh, rl) + one(ll, rh))


def exact(left, right, dims=(((1,), (0,)), ((), ()))):
    return lax.dot_general(
        left, right, dims, precision=lax.Precision.HIGHEST, preferred_element_type=jnp.float32
    )


def lane_roll(value, by):
    return pltpu.roll(value, by % value.shape[-1], axis=value.ndim - 1)


def lanes(shape):
    return lax.broadcasted_iota(jnp.int32, shape, len(shape) - 1)


AXES = ("gx", "gy", "gz")


def parities():
    return [lax.rem(lax.axis_index(axis), 2) for axis in AXES]


def place():
    a, b, c = parities()
    return CUBE - 1 - (a * 4 + b * 2 + c)


def cubes():
    sizes = [lax.axis_size(axis) for axis in AXES]
    groups = []
    for i in range(sizes[0] // 2):
        for j in range(sizes[1] // 2):
            for k in range(sizes[2] // 2):
                group = []
                for spot in range(CUBE):
                    at = [
                        (2 * base + 1 + (spot >> (2 - axis) & 1)) % sizes[axis]
                        for axis, base in enumerate((i, j, k))
                    ]
                    group.append((at[0] * sizes[1] + at[1]) * sizes[2] + at[2])
                groups.append(group)
    return groups


def swapped(shard, axis):
    return lax.ppermute(shard, axis, [(i, i ^ 1) for i in range(lax.axis_size(axis))])


def tiles_kernel(tiles_ref, peak_ref, wide_ref):
    ny = lax.axis_size("gy")
    nz = lax.axis_size("gz")
    gy = lax.axis_index("gy")
    gz = lax.axis_index("gz")
    py = lax.rem(gy + ny - 1, ny)
    pz = lax.rem(gz + nz - 1, nz)
    near = lanes((8, 128)) % 16 < 8
    peak_ref[...] = jnp.broadcast_to(jnp.max(tiles_ref[...]), peak_ref.shape)
    for half, row in enumerate((py, gy)):
        low = tiles_ref[row * nz + pz]
        high = tiles_ref[row * nz + gz]
        wide_ref[:, half * 128 : (half + 1) * 128] = jnp.where(near, low, lane_roll(high, 8))


def filter_kernel(wide_ref, below_ref, orbitals_ref, u0_ref, u1_ref, u2_ref, own_ref, w_ref):
    first_half = lanes((8, 128)) % 16 < 8

    def packed(even, odd):
        return jnp.where(first_half, lane_roll(even, -68)[:, :128], lane_roll(odd, -60)[:, :128])

    planes = {}
    for plane in range(3, 13):
        row = below_ref[plane : plane + 1] if plane < 8 else wide_ref[plane - 8 : plane - 7]
        planes[plane] = jnp.broadcast_to(row, (8, 256)) + (3.0 - SHIFT)
        w_ref[plane - 3] = planes[plane]
    for q in range(4):
        own_ref[:, q * 128 : (q + 1) * 128] = packed(planes[4 + 2 * q], planes[5 + 2 * q])

    def around(value):
        return (
            lane_roll(value, 1) + lane_roll(value, -1) + lane_roll(value, 16) + lane_roll(value, -16)
        )

    def filter_rows(step, carry):
        rows = pl.ds(pl.multiple_of(step * 8, 8), 8)
        start = {p: orbitals_ref[rows, p * 256 : (p + 1) * 256] for p in range(2, 14)}
        once = {}
        for p in range(3, 13):
            total = around(start[p]) + (start[p - 1] + start[p + 1])
            once[p] = w_ref[p - 3] * start[p] - 0.5 * total
        twice = {}
        for p in range(4, 12):
            total = around(once[p]) + (once[p - 1] + once[p + 1])
            twice[p] = w_ref[p - 3] * once[p] - 0.5 * total
        for q in range(4):
            at = slice(q * 128, (q + 1) * 128)
            u0_ref[rows, at] = packed(start[4 + 2 * q], start[5 + 2 * q])
            u1_ref[rows, at] = packed(once[4 + 2 * q], once[5 + 2 * q])
            u2_ref[rows, at] = packed(twice[4 + 2 * q], twice[5 + 2 * q])
        return carry

    lax.fori_loop(0, ROWS // 8, filter_rows, 0)


def store_traces(ft, value, *refs):
    traces = dot3(split(ft), split(value))
    for slot in range(3):
        refs[slot][...] = traces[slot * FLAT : (slot + 1) * FLAT]
    at = place()
    for slot, flip in ((3, 4), (4, 2), (5, 1)):
        refs[3][at ^ flip] = traces[slot * FLAT : (slot + 1) * FLAT]


def basis_kernel(peaks_ref, u0_ref, u1_ref, u2_ref, own_ref, vectors_ref,
                 df_ref, ft_ref, scal_ref, x_ref, y_ref, z_ref, cube_ref, bt_ref):
    top = 6.0 + jnp.max(peaks_ref[...])
    centre = (top + cutoff) / 2.0
    half_width = (top - cutoff) / 2.0
    scal_ref[0] = centre
    scal_ref[1] = half_width
    moved = SHIFT - centre
    start = u0_ref[...]
    square = u2_ref[...] + (2.0 * moved) * u1_ref[...] + (moved * moved) * start
    restricted = square * (2.0 / (half_width * half_width)) - start
    halves = split(restricted)
    intersection = exact(restricted, restricted, (((1,), (1,)), ((), ())))
    sigma = jnp.sqrt(jnp.sum(intersection * intersection))
    identity = (
        lax.broadcasted_iota(jnp.int32, (ROWS, ROWS), 0) == lanes((ROWS, ROWS))
    ).astype(jnp.float32)
    current = intersection / sigma
    factor = 1.5 * identity - 0.5 * current
    current = exact(current, factor)
    root = factor
    for step in range(NEWTON - 1):
        factor = 1.5 * identity - 0.5 * exact(root, current)
        if step < NEWTON - 2:
            current = exact(current, factor)
        root = exact(factor, root)
    root = root / jnp.sqrt(sigma)
    basis = dot3(split(root), halves)

    own = own_ref[:1] + SHIFT
    cell = lanes((ROWS, WIDTH))
    z = cell % 8
    y = cell // 16 % 8
    x = cell // 128 * 2 + cell // 8 % 2
    odd = x % 2 == 1

    def gate(ok, value):
        return jnp.where(ok, value, 0.0)

    total = gate(z > 0, lane_roll(basis, 1)) + gate(z < 7, lane_roll(basis, -1))
    total = total + gate(y > 0, lane_roll(basis, 16)) + gate(y < 7, lane_roll(basis, -16))
    total = total + jnp.where(odd, lane_roll(basis, 8), lane_roll(basis, -8))
    total = total + gate(
        (x > 0) & (x < 7), jnp.where(odd, lane_roll(basis, -120), lane_roll(basis, 120))
    )
    applied = own * basis - 0.5 * total
    diagonal = dot3(split(basis), split(applied), (((1,), (1,)), ((), ())))

    bt_ref[...] = jnp.concatenate([basis, jnp.zeros((128 - ROWS, WIDTH), jnp.float32)], axis=0).T
    lower = (
        jnp.concatenate([bt_ref[yy * 16 : yy * 16 + 8] for yy in range(8)], axis=0),
        jnp.concatenate([bt_ref[q * 128 : q * 128 + 16] for q in range(4)], axis=0),
        bt_ref[pl.ds(0, FLAT, stride=8)],
    )
    upper = (
        jnp.concatenate([bt_ref[392 + yy * 16 : 400 + yy * 16] for yy in range(8)], axis=0),
        jnp.concatenate([bt_ref[q * 128 + 112 : q * 128 + 128] for q in range(4)], axis=0),
        bt_ref[pl.ds(7, FLAT, stride=8)],
    )
    bits = parities()
    pieces = [jnp.where(bit == 0, u, l) for bit, u, l in zip(bits, upper, lower)]
    pieces += [jnp.where(bit == 0, l, u) for bit, u, l in zip(bits, upper, lower)]
    faces_t = jnp.concatenate(pieces, axis=0)
    ft = faces_t[:, :ROWS]
    ft_ref[...] = ft
    df_ref[:, :BODY] = -0.5 * faces_t.T[:ROWS]
    df_ref[:, BODY : BODY + ROWS] = diagonal
    df_ref[:, BODY + ROWS :] = jnp.zeros((ROWS, WIDTH - BODY - ROWS), jnp.float32)
    store_traces(ft, vectors_ref[...], x_ref, y_ref, z_ref, cube_ref)


def step_kernel(first, last, scal_ref, df_ref, ft_ref, now_ref, prior_ref, x_ref, y_ref, z_ref,
                cube_ref, out_ref, *sent):
    now = now_ref[...]
    at = place()
    halos = [x_ref[...], y_ref[...], z_ref[...]]
    halos += [cube_ref[at ^ flip] for flip in (4, 2, 1)]
    stacked = jnp.concatenate(
        halos + [now, jnp.zeros((WIDTH - BODY - ROWS, COLS), jnp.float32)], axis=0
    )
    result = dot3(split(df_ref[...]), split(stacked))
    centre, half_width = scal_ref[0], scal_ref[1]
    following = (result - centre * now) / half_width
    if not first:
        following = 2.0 * following - prior_ref[...]
    out_ref[...] = following
    if not last:
        store_traces(ft_ref[...], following, *sent)


def vmem():
    return pl.BlockSpec(memory_space=pltpu.VMEM)


def smem():
    return pl.BlockSpec(memory_space=pltpu.SMEM)


def of(*shape):
    return jax.ShapeDtypeStruct(shape, jnp.float32)


def per_device(orbitals, potential, coefficients):
    f32 = jnp.float32
    nx = lax.axis_size("gx")
    plane = lax.axis_size("gy") * lax.axis_size("gz")
    spread = jnp.pad(potential, ((0, 0), (0, 0), (0, 8))).reshape(8, 128)
    near = lanes((8, 128)) % 16 < 8
    block = jnp.where(near, spread, jnp.max(potential))
    tiles = lax.all_to_all(jnp.broadcast_to(block, (plane, 8, 128)), ("gy", "gz"), 0, 0)
    peak, wide = pl.pallas_call(
        tiles_kernel,
        out_shape=(of(nx, 1, 128), of(8, 256)),
        in_specs=[vmem()],
        out_specs=(vmem(), vmem()),
        compiler_params=pltpu.CompilerParams(vmem_limit_bytes=GRANT),
        name="tiles",
    )(tiles)
    peaks = lax.all_to_all(peak, "gx", 0, 0)
    below = shifted(wide, "gx", 1)
    powers = pl.pallas_call(
        filter_kernel,
        out_shape=(of(ROWS, WIDTH), of(ROWS, WIDTH), of(ROWS, WIDTH), of(8, WIDTH)),
        in_specs=[vmem(), vmem(), vmem()],
        out_specs=(vmem(),) * 4,
        scratch_shapes=[pltpu.VMEM((10, 8, 256), f32)],
        compiler_params=pltpu.CompilerParams(vmem_limit_bytes=GRANT),
        name="powers",
    )(wide, below, orbitals.reshape(ROWS, -1))
    start = coefficients.reshape(ROWS, COLS)
    sent_shapes = (of(FLAT, COLS),) * 3 + (of(CUBE, FLAT, COLS),)
    df, ft, scal, *sent = pl.pallas_call(
        basis_kernel,
        out_shape=(of(ROWS, WIDTH), of(BODY, ROWS), of(2)) + sent_shapes,
        in_specs=[vmem()] * 6,
        out_specs=(vmem(), vmem(), smem()) + (vmem(),) * 4,
        scratch_shapes=[pltpu.VMEM((WIDTH, 128), f32)],
        compiler_params=pltpu.CompilerParams(vmem_limit_bytes=GRANT),
        name="basis",
    )(peaks, *powers, start)

    groups = cubes()
    prior, now = start, start
    for step in range(DG_STEPS):
        halos = [swapped(trace, axis) for trace, axis in zip(sent, AXES)]
        halos.append(lax.all_to_all(sent[3], AXES, 0, 0, axis_index_groups=groups))
        last = step == DG_STEPS - 1
        shapes = (of(ROWS, COLS),) + (() if last else sent_shapes)

        def body(*refs, step=step, last=last):
            step_kernel(step == 0, last, *refs)

        following, *sent = pl.pallas_call(
            body,
            out_shape=shapes,
            in_specs=[smem()] + [vmem()] * 8,
            out_specs=tuple(vmem() for _ in shapes),
            compiler_params=pltpu.CompilerParams(vmem_limit_bytes=GRANT),
            name=f"step{step}",
        )(scal, df, ft, now, prior, *halos)
        prior, now = now, following
    return now.reshape(coefficients.shape)


def solution(mesh):
    placed = (P("gx", "gy", "gz", None, None), P("gx", "gy", "gz"), P("gx", "gy", "gz", None, None))
    return jax.shard_map(
        per_device,
        mesh=mesh,
        in_specs=placed,
        out_specs=P("gx", "gy", "gz", None, None),
        check_vma=False,
    )
```

```python
import jax
import jax.numpy as jnp
from jax import lax
from jax.experimental import pallas as pl
from jax.experimental.pallas import tpu as pltpu
from jax.sharding import PartitionSpec as P

NEWTON = 6
DG_STEPS = 3
SHIFT = 3.0
ROWS = 96
EDGE = 8
FLAT = EDGE * EDGE
COLS = 256
FACES = 6
RING = 4
GRANT = 16 << 20
BODY = FACES * FLAT
WIDTH = 512
cutoff = 1.0


def shifted(shard, axis, by):
    count = lax.axis_size(axis)
    return lax.ppermute(shard, axis, [(i, (i + by) % count) for i in range(count)])


def split(value):
    high = value.astype(jnp.bfloat16)
    low = (value - high.astype(jnp.float32)).astype(jnp.bfloat16)
    return high, low


def dot3(left, right, dims=(((1,), (0,)), ((), ()))):
    lh, ll = left
    rh, rl = right

    def one(a, b):
        return lax.dot_general(a, b, dims, preferred_element_type=jnp.float32)

    return one(lh, rh) + (one(lh, rl) + one(ll, rh))


def exact(left, right, dims=(((1,), (0,)), ((), ()))):
    return lax.dot_general(
        left, right, dims, precision=lax.Precision.HIGHEST, preferred_element_type=jnp.float32
    )


def lane_roll(value, by):
    return pltpu.roll(value, by % value.shape[-1], axis=value.ndim - 1)


def lanes(shape):
    return lax.broadcasted_iota(jnp.int32, shape, len(shape) - 1)


SWAPS = (("gz", 0), ("gx", 0), ("gy", 1), ("gy", 0))
SLOTS = SWAPS + (("gx", 1), ("gz", 1))
AXES = ("gx", "gy", "gz")


def upper_side(axis, odd):
    return lax.rem(lax.axis_index(axis), 2) == odd


def swapped(shard, axis, odd):
    count = lax.axis_size(axis)
    pairs = [((2 * i + odd) % count, (2 * i + 1 + odd) % count) for i in range(count // 2)]
    return lax.ppermute(shard, axis, pairs + [(b, a) for a, b in pairs])


def place():
    return (1 - lax.rem(lax.axis_index("gx"), 2)) * 2 + 1 - lax.rem(lax.axis_index("gz"), 2)


def rings():
    nx, nz = lax.axis_size("gx"), lax.axis_size("gz")
    return [
        [(2 * i + 1 + a) % nx * nz + (2 * k + 1 + c) % nz for a in range(2) for c in range(2)]
        for i in range(nx // 2)
        for k in range(nz // 2)
    ]


def tile_kernel(potential_ref, out_ref):
    lane = lanes((8, 128))
    tile = jnp.full((8, 128), jnp.max(potential_ref[...]))
    for y in range(8):
        row = jnp.concatenate([potential_ref[:, y, :], jnp.zeros((8, 120), jnp.float32)], axis=1)
        if y:
            row = lane_roll(row, 16 * y)
        tile = jnp.where((lane >= 16 * y) & (lane < 16 * y + 8), row, tile)
    out_ref[...] = jnp.broadcast_to(tile, out_ref.shape)


def tiles_kernel(tiles_ref, peak_ref, wide_ref):
    ny = lax.axis_size("gy")
    nz = lax.axis_size("gz")
    gy = lax.axis_index("gy")
    gz = lax.axis_index("gz")
    py = lax.rem(gy + ny - 1, ny)
    pz = lax.rem(gz + nz - 1, nz)
    near = lanes((8, 128)) % 16 < 8
    peak_ref[...] = jnp.broadcast_to(jnp.max(tiles_ref[...]), peak_ref.shape)
    for half, row in enumerate((py, gy)):
        low = tiles_ref[row * nz + pz]
        high = tiles_ref[row * nz + gz]
        wide_ref[:, half * 128 : (half + 1) * 128] = jnp.where(near, low, lane_roll(high, 8))


def filter_kernel(wide_ref, below_ref, orbitals_ref, u0_ref, u1_ref, u2_ref, own_ref, w_ref,
                  held_ref, sems):
    def fetch(step):
        rows = pl.ds(pl.multiple_of(step * 8, 8), 8)
        return pltpu.make_async_copy(orbitals_ref.at[rows], held_ref.at[step], sems.at[step])

    for step in range(ROWS // 8):
        fetch(step).start()
    first_half = lanes((8, 128)) % 16 < 8

    def packed(even, odd):
        return jnp.where(first_half, lane_roll(even, -68)[:, :128], lane_roll(odd, -60)[:, :128])

    planes = {}
    for plane in range(3, 13):
        row = below_ref[plane : plane + 1] if plane < 8 else wide_ref[plane - 8 : plane - 7]
        planes[plane] = jnp.broadcast_to(row, (8, 256)) + (3.0 - SHIFT)
        w_ref[plane - 3] = planes[plane]
    for q in range(4):
        own_ref[:, q * 128 : (q + 1) * 128] = packed(planes[4 + 2 * q], planes[5 + 2 * q])

    def around(value):
        return (
            lane_roll(value, 1) + lane_roll(value, -1) + lane_roll(value, 16) + lane_roll(value, -16)
        )

    def filter_rows(step, carry):
        rows = pl.ds(pl.multiple_of(step * 8, 8), 8)
        fetch(step).wait()
        start = {p: held_ref[step, :, p * 256 : (p + 1) * 256] for p in range(2, 14)}
        once = {}
        for p in range(3, 13):
            total = around(start[p]) + (start[p - 1] + start[p + 1])
            once[p] = w_ref[p - 3] * start[p] - 0.5 * total
        twice = {}
        for p in range(4, 12):
            total = around(once[p]) + (once[p - 1] + once[p + 1])
            twice[p] = w_ref[p - 3] * once[p] - 0.5 * total
        for q in range(4):
            at = slice(q * 128, (q + 1) * 128)
            u0_ref[rows, at] = packed(start[4 + 2 * q], start[5 + 2 * q])
            u1_ref[rows, at] = packed(once[4 + 2 * q], once[5 + 2 * q])
            u2_ref[rows, at] = packed(twice[4 + 2 * q], twice[5 + 2 * q])
        return carry

    lax.fori_loop(0, ROWS // 8, filter_rows, 0)


def store_traces(ft, value, *refs):
    traces = dot3(split(ft), split(value))
    for slot in range(4):
        refs[slot][...] = traces[slot * FLAT : (slot + 1) * FLAT]
    at = place()
    for slot, flip in ((4, 2), (5, 1)):
        refs[4][at ^ flip] = traces[slot * FLAT : (slot + 1) * FLAT]


def basis_kernel(peaks_ref, u0_ref, u1_ref, u2_ref, own_ref, vectors_ref,
                 df_ref, ft_ref, scal_ref, *refs):
    sent, bt_ref = refs[:-1], refs[-1]
    top = 6.0 + jnp.max(peaks_ref[...])
    centre = (top + cutoff) / 2.0
    half_width = (top - cutoff) / 2.0
    scal_ref[0] = centre
    scal_ref[1] = half_width
    moved = SHIFT - centre
    start = u0_ref[...]
    square = u2_ref[...] + (2.0 * moved) * u1_ref[...] + (moved * moved) * start
    restricted = square * (2.0 / (half_width * half_width)) - start
    halves = split(restricted)
    intersection = exact(restricted, restricted, (((1,), (1,)), ((), ())))
    sigma = jnp.sqrt(jnp.sum(intersection * intersection))
    identity = (
        lax.broadcasted_iota(jnp.int32, (ROWS, ROWS), 0) == lanes((ROWS, ROWS))
    ).astype(jnp.float32)
    current = intersection / sigma
    factor = 1.5 * identity - 0.5 * current
    current = exact(current, factor)
    root = factor
    for step in range(NEWTON - 1):
        factor = 1.5 * identity - 0.5 * exact(root, current)
        if step < NEWTON - 2:
            current = exact(current, factor)
        root = exact(factor, root)
    root = root / jnp.sqrt(sigma)
    basis = dot3(split(root), halves)

    own = own_ref[:1] + SHIFT
    cell = lanes((ROWS, WIDTH))
    z = cell % 8
    y = cell // 16 % 8
    x = cell // 128 * 2 + cell // 8 % 2
    odd = x % 2 == 1

    def gate(ok, value):
        return jnp.where(ok, value, 0.0)

    total = gate(z > 0, lane_roll(basis, 1)) + gate(z < 7, lane_roll(basis, -1))
    total = total + gate(y > 0, lane_roll(basis, 16)) + gate(y < 7, lane_roll(basis, -16))
    total = total + jnp.where(odd, lane_roll(basis, 8), lane_roll(basis, -8))
    total = total + gate(
        (x > 0) & (x < 7), jnp.where(odd, lane_roll(basis, -120), lane_roll(basis, 120))
    )
    applied = own * basis - 0.5 * total
    diagonal = dot3(split(basis), split(applied), (((1,), (1,)), ((), ())))

    bt_ref[...] = jnp.concatenate([basis, jnp.zeros((128 - ROWS, WIDTH), jnp.float32)], axis=0).T
    lower = (
        jnp.concatenate([bt_ref[yy * 16 : yy * 16 + 8] for yy in range(8)], axis=0),
        jnp.concatenate([bt_ref[q * 128 : q * 128 + 16] for q in range(4)], axis=0),
        bt_ref[pl.ds(0, FLAT, stride=8)],
    )
    upper = (
        jnp.concatenate([bt_ref[392 + yy * 16 : 400 + yy * 16] for yy in range(8)], axis=0),
        jnp.concatenate([bt_ref[q * 128 + 112 : q * 128 + 128] for q in range(4)], axis=0),
        bt_ref[pl.ds(7, FLAT, stride=8)],
    )
    pieces = [
        jnp.where(upper_side(axis, odd), upper[AXES.index(axis)], lower[AXES.index(axis)])
        for axis, odd in SLOTS
    ]
    faces_t = jnp.concatenate(pieces, axis=0)
    ft = faces_t[:, :ROWS]
    ft_ref[...] = ft
    df_ref[:, :BODY] = -0.5 * faces_t.T[:ROWS]
    df_ref[:, BODY : BODY + ROWS] = diagonal
    df_ref[:, BODY + ROWS :] = jnp.zeros((ROWS, WIDTH - BODY - ROWS), jnp.float32)
    store_traces(ft, vectors_ref[...], *sent)


def step_kernel(first, last, scal_ref, df_ref, ft_ref, now_ref, prior_ref, *refs):
    swap_refs, ring_ref, out_ref, sent = refs[:4], refs[4], refs[5], refs[6:]
    now = now_ref[...]
    at = place()
    halos = [ref[...] for ref in swap_refs] + [ring_ref[at ^ 2], ring_ref[at ^ 1]]
    stacked = jnp.concatenate(
        halos + [now, jnp.zeros((WIDTH - BODY - ROWS, COLS), jnp.float32)], axis=0
    )
    result = dot3(split(df_ref[...]), split(stacked))
    centre, half_width = scal_ref[0], scal_ref[1]
    following = (result - centre * now) / half_width
    if not first:
        following = 2.0 * following - prior_ref[...]
    out_ref[...] = following
    if not last:
        store_traces(ft_ref[...], following, *sent)


def vmem():
    return pl.BlockSpec(memory_space=pltpu.VMEM)


def smem():
    return pl.BlockSpec(memory_space=pltpu.SMEM)


def of(*shape):
    return jax.ShapeDtypeStruct(shape, jnp.float32)


def per_device(orbitals, potential, coefficients):
    f32 = jnp.float32
    nx = lax.axis_size("gx")
    plane = lax.axis_size("gy") * lax.axis_size("gz")
    tile = pl.pallas_call(
        tile_kernel,
        out_shape=of(plane, 8, 128),
        in_specs=[vmem()],
        out_specs=vmem(),
        compiler_params=pltpu.CompilerParams(vmem_limit_bytes=GRANT),
        name="tile",
    )(potential)
    tiles = lax.all_to_all(tile, ("gy", "gz"), 0, 0)
    peak, wide = pl.pallas_call(
        tiles_kernel,
        out_shape=(of(nx, 1, 128), of(8, 256)),
        in_specs=[vmem()],
        out_specs=(vmem(), vmem()),
        compiler_params=pltpu.CompilerParams(vmem_limit_bytes=GRANT),
        name="tiles",
    )(tiles)
    peaks = lax.all_to_all(peak, "gx", 0, 0)
    below = shifted(wide, "gx", 1)
    powers = pl.pallas_call(
        filter_kernel,
        out_shape=(of(ROWS, WIDTH), of(ROWS, WIDTH), of(ROWS, WIDTH), of(8, WIDTH)),
        in_specs=[vmem(), vmem(), pl.BlockSpec(memory_space=pltpu.HBM)],
        out_specs=(vmem(),) * 4,
        scratch_shapes=[
            pltpu.VMEM((10, 8, 256), f32),
            pltpu.VMEM((ROWS // 8, 8, 4096), f32),
            pltpu.SemaphoreType.DMA((ROWS // 8,)),
        ],
        compiler_params=pltpu.CompilerParams(vmem_limit_bytes=GRANT),
        name="powers",
    )(wide, below, orbitals.reshape(ROWS, -1))
    start = coefficients.reshape(ROWS, COLS)
    sent_shapes = (of(FLAT, COLS),) * 4 + (of(RING, FLAT, COLS),)
    df, ft, scal, *sent = pl.pallas_call(
        basis_kernel,
        out_shape=(of(ROWS, WIDTH), of(BODY, ROWS), of(2)) + sent_shapes,
        in_specs=[vmem()] * 6,
        out_specs=(vmem(), vmem(), smem()) + (vmem(),) * 5,
        scratch_shapes=[pltpu.VMEM((WIDTH, 128), f32)],
        compiler_params=pltpu.CompilerParams(vmem_limit_bytes=GRANT),
        name="basis",
    )(peaks, *powers, start)

    groups = rings()
    prior, now = start, start
    for step in range(DG_STEPS):
        halos = [swapped(trace, *pairing) for trace, pairing in zip(sent, SWAPS)]
        halos.append(lax.all_to_all(sent[4], ("gx", "gz"), 0, 0, axis_index_groups=groups))
        last = step == DG_STEPS - 1
        shapes = (of(ROWS, COLS),) + (() if last else sent_shapes)

        def body(*refs, step=step, last=last):
            step_kernel(step == 0, last, *refs)

        following, *sent = pl.pallas_call(
            body,
            out_shape=shapes,
            in_specs=[smem()] + [vmem()] * 9,
            out_specs=tuple(vmem() for _ in shapes),
            compiler_params=pltpu.CompilerParams(vmem_limit_bytes=GRANT),
            name=f"step{step}",
        )(scal, df, ft, now, prior, *halos)
        prior, now = now, following
    return now.reshape(coefficients.shape)


def solution(mesh):
    placed = (P("gx", "gy", "gz", None, None), P("gx", "gy", "gz"), P("gx", "gy", "gz", None, None))
    return jax.shard_map(
        per_device,
        mesh=mesh,
        in_specs=placed,
        out_specs=P("gx", "gy", "gz", None, None),
        check_vma=False,
    )
```

```python
import jax
import jax.numpy as jnp
from jax import lax
from jax.experimental import pallas as pl
from jax.experimental.pallas import tpu as pltpu
from jax.sharding import PartitionSpec as P

NEWTON = 6
DG_STEPS = 3
SHIFT = 3.0
ROWS = 96
EDGE = 8
FLAT = EDGE * EDGE
COLS = 256
FACES = 6
CUBE = 8
GRANT = 16 << 20
BODY = FACES * FLAT
WIDTH = 512
cutoff = 1.0


def shifted(shard, axis, by):
    count = lax.axis_size(axis)
    return lax.ppermute(shard, axis, [(i, (i + by) % count) for i in range(count)])


def split(value):
    high = value.astype(jnp.bfloat16)
    low = (value - high.astype(jnp.float32)).astype(jnp.bfloat16)
    return high, low


def dot3(left, right, dims=(((1,), (0,)), ((), ()))):
    lh, ll = left
    rh, rl = right
    rows = lh.shape[0]

    def one(a, b):
        return lax.dot_general(a, b, dims, preferred_element_type=jnp.float32)

    both = one(jnp.concatenate([lh, ll], axis=0), rh)
    return both[:rows] + (both[rows:] + one(lh, rl))


def exact(left, right, dims=(((1,), (0,)), ((), ()))):
    return lax.dot_general(
        left, right, dims, precision=lax.Precision.HIGHEST, preferred_element_type=jnp.float32
    )


def product(left, right):
    return dot3(split(left), split(right))


def lane_roll(value, by):
    return pltpu.roll(value, by % value.shape[-1], axis=value.ndim - 1)


def lanes(shape):
    return lax.broadcasted_iota(jnp.int32, shape, len(shape) - 1)


SWAPS = (("gz", 1), ("gx", 1), ("gy", 1))
AXES = ("gx", "gy", "gz")
SLOTS = SWAPS + tuple((axis, 0) for axis in AXES)
FLIPS = (4, 2, 1)


def upper_side(axis, odd):
    return lax.rem(lax.axis_index(axis), 2) == odd


def swapped(shard, axis, odd):
    count = lax.axis_size(axis)
    pairs = [((2 * i + odd) % count, (2 * i + 1 + odd) % count) for i in range(count // 2)]
    return lax.ppermute(shard, axis, pairs + [(b, a) for a, b in pairs])


def place():
    return sum(flip * lax.rem(lax.axis_index(axis), 2) for flip, axis in zip(FLIPS, AXES))


def cubes():
    nx, ny, nz = (lax.axis_size(axis) for axis in AXES)
    return [
        [
            ((2 * i + a) * ny + 2 * j + b) * nz + 2 * k + c
            for a in range(2)
            for b in range(2)
            for c in range(2)
        ]
        for i in range(nx // 2)
        for j in range(ny // 2)
        for k in range(nz // 2)
    ]


def tile_kernel(potential_ref, out_ref):
    lane = lanes((8, 128))
    tile = jnp.full((8, 128), jnp.max(potential_ref[...]))
    for y in range(8):
        row = jnp.concatenate([potential_ref[:, y, :], jnp.zeros((8, 120), jnp.float32)], axis=1)
        if y:
            row = lane_roll(row, 16 * y)
        tile = jnp.where((lane >= 16 * y) & (lane < 16 * y + 8), row, tile)
    out_ref[...] = jnp.broadcast_to(tile, out_ref.shape)


def tiles_kernel(tiles_ref, peak_ref, wide_ref):
    ny = lax.axis_size("gy")
    nz = lax.axis_size("gz")
    gy = lax.axis_index("gy")
    gz = lax.axis_index("gz")
    py = lax.rem(gy + ny - 1, ny)
    pz = lax.rem(gz + nz - 1, nz)
    near = lanes((8, 128)) % 16 < 8
    peak_ref[...] = jnp.broadcast_to(jnp.max(tiles_ref[...]), peak_ref.shape)
    for half, row in enumerate((py, gy)):
        low = tiles_ref[row * nz + pz]
        high = tiles_ref[row * nz + gz]
        wide_ref[:, half * 128 : (half + 1) * 128] = jnp.where(near, low, lane_roll(high, 8))


def filter_kernel(wide_ref, below_ref, orbitals_ref, u0_ref, u1_ref, u2_ref, own_ref, w_ref):
    first_half = lanes((8, 128)) % 16 < 8

    def packed(even, odd):
        return jnp.where(first_half, lane_roll(even, -68)[:, :128], lane_roll(odd, -60)[:, :128])

    planes = {}
    for plane in range(3, 13):
        row = below_ref[plane : plane + 1] if plane < 8 else wide_ref[plane - 8 : plane - 7]
        planes[plane] = jnp.broadcast_to(row, (8, 256)) + (3.0 - SHIFT)
        w_ref[plane - 3] = planes[plane]
    for q in range(4):
        own_ref[:, q * 128 : (q + 1) * 128] = packed(planes[4 + 2 * q], planes[5 + 2 * q])

    def around(value):
        return (
            lane_roll(value, 1) + lane_roll(value, -1) + lane_roll(value, 16) + lane_roll(value, -16)
        )

    def filter_rows(step, carry):
        rows = pl.ds(pl.multiple_of(step * 8, 8), 8)
        start = {p: orbitals_ref[rows, p * 256 : (p + 1) * 256] for p in range(2, 14)}
        once = {}
        for p in range(3, 13):
            total = around(start[p]) + (start[p - 1] + start[p + 1])
            once[p] = w_ref[p - 3] * start[p] - 0.5 * total
        twice = {}
        for p in range(4, 12):
            total = around(once[p]) + (once[p - 1] + once[p + 1])
            twice[p] = w_ref[p - 3] * once[p] - 0.5 * total
        for q in range(4):
            at = slice(q * 128, (q + 1) * 128)
            u0_ref[rows, at] = packed(start[4 + 2 * q], start[5 + 2 * q])
            u1_ref[rows, at] = packed(once[4 + 2 * q], once[5 + 2 * q])
            u2_ref[rows, at] = packed(twice[4 + 2 * q], twice[5 + 2 * q])
        return carry

    lax.fori_loop(0, ROWS // 8, filter_rows, 0)


def store_traces(ft, value, *refs):
    right = split(value)
    half = BODY // 2
    for part in range(2):
        traces = dot3(split(ft[part * half : (part + 1) * half]), right)
        at = place()
        for slot in range(3):
            block = traces[slot * FLAT : (slot + 1) * FLAT]
            if part == 0:
                refs[slot][...] = block
            else:
                refs[3][at ^ FLIPS[slot]] = block


def basis_kernel(peaks_ref, u0_ref, u1_ref, u2_ref, own_ref, vectors_ref,
                 df_ref, ft_ref, scal_ref, *refs):
    sent, bt_ref = refs[:-1], refs[-1]
    top = 6.0 + jnp.max(peaks_ref[...])
    centre = (top + cutoff) / 2.0
    half_width = (top - cutoff) / 2.0
    scal_ref[0] = centre
    scal_ref[1] = half_width
    moved = SHIFT - centre
    start = u0_ref[...]
    square = u2_ref[...] + (2.0 * moved) * u1_ref[...] + (moved * moved) * start
    restricted = square * (2.0 / (half_width * half_width)) - start
    halves = split(restricted)
    intersection = dot3(halves, halves, (((1,), (1,)), ((), ())))
    sigma = jnp.sqrt(jnp.sum(intersection * intersection))
    identity = (
        lax.broadcasted_iota(jnp.int32, (ROWS, ROWS), 0) == lanes((ROWS, ROWS))
    ).astype(jnp.float32)
    current = intersection / sigma
    factor = 1.5 * identity - 0.5 * current
    current = product(current, factor)
    root = factor
    for step in range(NEWTON - 1):
        factor = 1.5 * identity - 0.5 * product(root, current)
        if step < NEWTON - 2:
            current = product(current, factor)
        root = product(factor, root)
    root = root / jnp.sqrt(sigma)
    basis = dot3(split(root), halves)

    own = own_ref[:1] + SHIFT
    cell = lanes((ROWS, WIDTH))
    z = cell % 8
    y = cell // 16 % 8
    x = cell // 128 * 2 + cell // 8 % 2
    odd = x % 2 == 1

    def gate(ok, value):
        return jnp.where(ok, value, 0.0)

    total = gate(z > 0, lane_roll(basis, 1)) + gate(z < 7, lane_roll(basis, -1))
    total = total + gate(y > 0, lane_roll(basis, 16)) + gate(y < 7, lane_roll(basis, -16))
    total = total + jnp.where(odd, lane_roll(basis, 8), lane_roll(basis, -8))
    total = total + gate(
        (x > 0) & (x < 7), jnp.where(odd, lane_roll(basis, -120), lane_roll(basis, 120))
    )
    applied = own * basis - 0.5 * total
    diagonal = dot3(split(basis), split(applied), (((1,), (1,)), ((), ())))

    bt_ref[...] = jnp.concatenate([basis, jnp.zeros((128 - ROWS, WIDTH), jnp.float32)], axis=0).T
    lower = (
        jnp.concatenate([bt_ref[yy * 16 : yy * 16 + 8] for yy in range(8)], axis=0),
        jnp.concatenate([bt_ref[q * 128 : q * 128 + 16] for q in range(4)], axis=0),
        bt_ref[pl.ds(0, FLAT, stride=8)],
    )
    upper = (
        jnp.concatenate([bt_ref[392 + yy * 16 : 400 + yy * 16] for yy in range(8)], axis=0),
        jnp.concatenate([bt_ref[q * 128 + 112 : q * 128 + 128] for q in range(4)], axis=0),
        bt_ref[pl.ds(7, FLAT, stride=8)],
    )
    pieces = [
        jnp.where(upper_side(axis, odd), upper[AXES.index(axis)], lower[AXES.index(axis)])
        for axis, odd in SLOTS
    ]
    faces_t = jnp.concatenate(pieces, axis=0)
    ft = faces_t[:, :ROWS]
    ft_ref[...] = ft
    df_ref[:, :BODY] = -0.5 * faces_t.T[:ROWS]
    df_ref[:, BODY : BODY + ROWS] = diagonal
    df_ref[:, BODY + ROWS :] = jnp.zeros((ROWS, WIDTH - BODY - ROWS), jnp.float32)
    store_traces(ft, vectors_ref[...], *sent)


def step_kernel(first, last, scal_ref, df_ref, ft_ref, now_ref, prior_ref, *refs):
    swap_refs, cube_ref, out_ref, sent = refs[:3], refs[3], refs[4], refs[5:]
    now = now_ref[...]
    at = place()
    halos = [ref[...] for ref in swap_refs] + [cube_ref[at ^ flip] for flip in FLIPS]
    first_half = halos[:4]
    second_half = halos[4:] + [now, jnp.zeros((WIDTH - BODY - ROWS, COLS), jnp.float32)]
    result = dot3(
        split(df_ref[:, : WIDTH // 2]), split(jnp.concatenate(first_half, axis=0))
    ) + dot3(split(df_ref[:, WIDTH // 2 :]), split(jnp.concatenate(second_half, axis=0)))
    centre, half_width = scal_ref[0], scal_ref[1]
    following = (result - centre * now) / half_width
    if not first:
        following = 2.0 * following - prior_ref[...]
    out_ref[...] = following
    if not last:
        store_traces(ft_ref[...], following, *sent)


def vmem():
    return pl.BlockSpec(memory_space=pltpu.VMEM)


def smem():
    return pl.BlockSpec(memory_space=pltpu.SMEM)


def of(*shape):
    return jax.ShapeDtypeStruct(shape, jnp.float32)


def per_device(orbitals, potential, coefficients):
    f32 = jnp.float32
    nx = lax.axis_size("gx")
    plane = lax.axis_size("gy") * lax.axis_size("gz")
    tile = pl.pallas_call(
        tile_kernel,
        out_shape=of(plane, 8, 128),
        in_specs=[vmem()],
        out_specs=vmem(),
        compiler_params=pltpu.CompilerParams(vmem_limit_bytes=GRANT),
        name="tile",
    )(potential)
    tiles = lax.all_to_all(tile, ("gy", "gz"), 0, 0)
    peak, wide = pl.pallas_call(
        tiles_kernel,
        out_shape=(of(nx, 1, 128), of(8, 256)),
        in_specs=[vmem()],
        out_specs=(vmem(), vmem()),
        compiler_params=pltpu.CompilerParams(vmem_limit_bytes=GRANT),
        name="tiles",
    )(tiles)
    peaks = lax.all_to_all(peak, "gx", 0, 0)
    below = shifted(wide, "gx", 1)
    powers = pl.pallas_call(
        filter_kernel,
        out_shape=(of(ROWS, WIDTH), of(ROWS, WIDTH), of(ROWS, WIDTH), of(8, WIDTH)),
        in_specs=[vmem(), vmem(), vmem()],
        out_specs=(vmem(),) * 4,
        scratch_shapes=[pltpu.VMEM((10, 8, 256), f32)],
        compiler_params=pltpu.CompilerParams(vmem_limit_bytes=GRANT),
        name="powers",
    )(wide, below, orbitals.reshape(ROWS, -1))
    start = coefficients.reshape(ROWS, COLS)
    sent_shapes = (of(FLAT, COLS),) * 3 + (of(CUBE, FLAT, COLS),)
    df, ft, scal, *sent = pl.pallas_call(
        basis_kernel,
        out_shape=(of(ROWS, WIDTH), of(BODY, ROWS), of(2)) + sent_shapes,
        in_specs=[vmem()] * 6,
        out_specs=(vmem(), vmem(), smem()) + (vmem(),) * 4,
        scratch_shapes=[pltpu.VMEM((WIDTH, 128), f32)],
        compiler_params=pltpu.CompilerParams(vmem_limit_bytes=GRANT),
        name="basis",
    )(peaks, *powers, start)

    groups = cubes()
    prior, now = start, start
    for step in range(DG_STEPS):
        halos = [swapped(trace, *pairing) for trace, pairing in zip(sent, SWAPS)]
        halos.append(lax.all_to_all(sent[3], AXES, 0, 0, axis_index_groups=groups))
        last = step == DG_STEPS - 1
        shapes = (of(ROWS, COLS),) + (() if last else sent_shapes)

        def body(*refs, step=step, last=last):
            step_kernel(step == 0, last, *refs)

        following, *sent = pl.pallas_call(
            body,
            out_shape=shapes,
            in_specs=[smem()] + [vmem()] * 8,
            out_specs=tuple(vmem() for _ in shapes),
            compiler_params=pltpu.CompilerParams(vmem_limit_bytes=GRANT),
            name=f"step{step}",
        )(scal, df, ft, now, prior, *halos)
        prior, now = now, following
    return now.reshape(coefficients.shape)


def solution(mesh):
    placed = (P("gx", "gy", "gz", None, None), P("gx", "gy", "gz"), P("gx", "gy", "gz", None, None))
    return jax.shard_map(
        per_device,
        mesh=mesh,
        in_specs=placed,
        out_specs=P("gx", "gy", "gz", None, None),
        check_vma=False,
    )
```

```python
import jax
import jax.numpy as jnp
from jax import lax
from jax.experimental import pallas as pl
from jax.experimental.pallas import tpu as pltpu
from jax.sharding import PartitionSpec as P

NEWTON = 6
DG_STEPS = 3
ROWS = 96
EDGE = 8
FLAT = EDGE * EDGE
COLS = 256
FACES = 6
CUBE = 8
GRANT = 16 << 20
BODY = FACES * FLAT
WIDTH = 512
cutoff = 1.0


def shifted(shard, axis, by):
    count = lax.axis_size(axis)
    return lax.ppermute(shard, axis, [(i, (i + by) % count) for i in range(count)])


def split(value):
    high = value.astype(jnp.bfloat16)
    low = (value - high.astype(jnp.float32)).astype(jnp.bfloat16)
    return high, low


def dot3(left, right, dims=(((1,), (0,)), ((), ()))):
    lh, ll = left
    rh, rl = right
    rows = lh.shape[0]

    def one(a, b):
        return lax.dot_general(a, b, dims, preferred_element_type=jnp.float32)

    both = one(jnp.concatenate([lh, ll], axis=0), rh)
    return both[:rows] + (both[rows:] + one(lh, rl))


def exact(left, right, dims=(((1,), (0,)), ((), ()))):
    return lax.dot_general(
        left, right, dims, precision=lax.Precision.HIGHEST, preferred_element_type=jnp.float32
    )


def product(left, right):
    return dot3(split(left), split(right))


def lane_roll(value, by):
    return pltpu.roll(value, by % value.shape[-1], axis=value.ndim - 1)


def lanes(shape):
    return lax.broadcasted_iota(jnp.int32, shape, len(shape) - 1)


SWAPS = (("gz", 1), ("gx", 1), ("gy", 0))
CUBE_PAIRS = (("gx", 0), ("gy", 1), ("gz", 0))
SLOTS = SWAPS + CUBE_PAIRS
AXES = ("gx", "gy", "gz")
FLIPS = (4, 2, 1)


def upper_side(axis, odd):
    return lax.rem(lax.axis_index(axis), 2) == odd


def swapped(shard, axis, odd):
    count = lax.axis_size(axis)
    pairs = [((2 * i + odd) % count, (2 * i + 1 + odd) % count) for i in range(count // 2)]
    return lax.ppermute(shard, axis, pairs + [(b, a) for a, b in pairs])


def place():
    return sum(
        flip * lax.rem(lax.axis_index(axis) + odd, 2) for flip, (axis, odd) in zip(FLIPS, CUBE_PAIRS)
    )


def cubes():
    sizes = [lax.axis_size(axis) for axis in AXES]
    groups = []
    for base in ((i, j, k) for i in range(sizes[0] // 2) for j in range(sizes[1] // 2) for k in range(sizes[2] // 2)):
        group = []
        for spot in range(CUBE):
            x, y, z = [
                (2 * base[n] + CUBE_PAIRS[n][1] + (spot // FLIPS[n]) % 2) % sizes[n] for n in range(3)
            ]
            group.append((x * sizes[1] + y) * sizes[2] + z)
        groups.append(group)
    return groups


def tile_kernel(potential_ref, tile_ref, peak_ref):
    lane = lanes((8, 128))
    potential = potential_ref[...]
    tile = jnp.zeros((8, 128), jnp.float32)
    for y in range(8):
        row = jnp.concatenate([potential_ref[:, y, :], jnp.zeros((8, 120), jnp.float32)], axis=1)
        if y:
            row = lane_roll(row, 16 * y)
        tile = jnp.where((lane >= 16 * y) & (lane < 16 * y + 8), row, tile)
    tile_ref[...] = tile
    peak_ref[...] = jnp.broadcast_to(jnp.max(potential), peak_ref.shape)


def block_kernel(tile_ref, below_ref, peaks_ref, out_ref):
    shape = (8, 128)
    near = lanes(shape) % 16 < 8
    row = lax.broadcasted_iota(jnp.int32, shape, 0)
    block = jnp.where(row == 5, jnp.max(peaks_ref[...]), tile_ref[...])
    block = jnp.where(near, block, lane_roll(below_ref[...], 8))
    out_ref[...] = jnp.broadcast_to(block, out_ref.shape)


def send_traces(ft, value, sent, held_ref, sems):
    right = split(value)
    half = BODY // 2
    traces = dot3(split(ft[half:]), right)
    at = place()
    copies = []
    for n, flip in enumerate(FLIPS):
        held_ref[n] = traces[n * FLAT : (n + 1) * FLAT]
        copies.append(pltpu.make_async_copy(held_ref.at[n], sent[3].at[at ^ flip], sems.at[n]))
        copies[-1].start()
    traces = dot3(split(ft[:half]), right)
    for slot in range(3):
        sent[slot][...] = traces[slot * FLAT : (slot + 1) * FLAT]
    for copy in copies:
        copy.wait()


def basis_kernel(tiles_ref, orbitals_ref, vectors_ref, df_ref, ft_ref, scal_ref, *refs):
    sent, (w_ref, restricted_ref, bt_ref, held_ref, sems) = refs[:-5], refs[-5:]
    gy = lax.axis_index("gy")
    gz = lax.axis_index("gz")
    ny = lax.axis_size("gy")
    nz = lax.axis_size("gz")
    py = lax.rem(gy + ny - 1, ny)
    pz = lax.rem(gz + nz - 1, nz)
    near = lanes((8, 128)) % 16 < 8
    tallest = jnp.max(jnp.max(tiles_ref[...], axis=0)[5:6])
    top = 6.0 + tallest
    centre = (top + cutoff) / 2.0
    half_width = (top - cutoff) / 2.0
    scal_ref[0] = centre
    scal_ref[1] = half_width
    own_x, prior_x = [], []
    for row in (py, gy):
        low = tiles_ref[row * nz + pz]
        high = tiles_ref[row * nz + gz]
        own_x.append(jnp.where(near, low, lane_roll(high, 8)))
        prior_x.append(jnp.where(near, lane_roll(low, -8), high))
    own_x = jnp.concatenate(own_x, axis=1)
    prior_x = jnp.concatenate(prior_x, axis=1)
    planes = {}
    for plane in range(3, 13):
        source, row = (prior_x, plane) if plane < 8 else (own_x, plane - 8)
        planes[plane] = jnp.broadcast_to(source[row : row + 1], (8, 256))
        w_ref[plane - 3] = planes[plane] + (3.0 - centre)
    first_half = lanes((8, 128)) % 16 < 8

    def packed(even, odd):
        return jnp.where(first_half, lane_roll(even, -68)[:, :128], lane_roll(odd, -60)[:, :128])

    inverse = 1.0 / half_width

    def around(value):
        return (
            lane_roll(value, 1) + lane_roll(value, -1) + lane_roll(value, 16) + lane_roll(value, -16)
        )

    def filter_rows(step, carry):
        rows = pl.ds(pl.multiple_of(step * 8, 8), 8)
        start = {p: orbitals_ref[rows, p * 256 : (p + 1) * 256] for p in range(2, 14)}
        once = {}
        for p in range(3, 13):
            total = around(start[p]) + (start[p - 1] + start[p + 1])
            once[p] = (w_ref[p - 3] * start[p] - 0.5 * total) * inverse
        twice = {}
        for p in range(4, 12):
            total = around(once[p]) + (once[p - 1] + once[p + 1])
            twice[p] = (w_ref[p - 3] * once[p] - 0.5 * total) * (2.0 * inverse) - start[p]
        for q in range(4):
            restricted_ref[rows, q * 128 : (q + 1) * 128] = packed(twice[4 + 2 * q], twice[5 + 2 * q])
        return carry

    lax.fori_loop(0, ROWS // 8, filter_rows, 0)
    restricted = restricted_ref[...]
    halves = split(restricted)
    intersection = dot3(halves, halves, (((1,), (1,)), ((), ())))
    sigma = jnp.sqrt(jnp.sum(intersection * intersection))
    identity = (
        lax.broadcasted_iota(jnp.int32, (ROWS, ROWS), 0) == lanes((ROWS, ROWS))
    ).astype(jnp.float32)
    current = intersection / sigma
    factor = 1.5 * identity - 0.5 * current
    current = product(current, factor)
    root = factor
    for step in range(NEWTON - 1):
        factor = 1.5 * identity - 0.5 * product(root, current)
        if step < NEWTON - 2:
            current = product(current, factor)
        root = product(factor, root)
    root = root / jnp.sqrt(sigma)
    basis = dot3(split(root), halves)

    own = jnp.concatenate([packed(planes[4 + 2 * q], planes[5 + 2 * q]) for q in range(4)], axis=1)
    own = own[:1] + 3.0
    cell = lanes((ROWS, WIDTH))
    z = cell % 8
    y = cell // 16 % 8
    x = cell // 128 * 2 + cell // 8 % 2
    odd = x % 2 == 1

    def gate(ok, value):
        return jnp.where(ok, value, 0.0)

    total = gate(z > 0, lane_roll(basis, 1)) + gate(z < 7, lane_roll(basis, -1))
    total = total + gate(y > 0, lane_roll(basis, 16)) + gate(y < 7, lane_roll(basis, -16))
    total = total + jnp.where(odd, lane_roll(basis, 8), lane_roll(basis, -8))
    total = total + gate(
        (x > 0) & (x < 7), jnp.where(odd, lane_roll(basis, -120), lane_roll(basis, 120))
    )
    applied = own * basis - 0.5 * total
    diagonal = dot3(split(basis), split(applied), (((1,), (1,)), ((), ())))

    bt_ref[...] = jnp.concatenate([basis, jnp.zeros((128 - ROWS, WIDTH), jnp.float32)], axis=0).T
    lower = (
        jnp.concatenate([bt_ref[yy * 16 : yy * 16 + 8] for yy in range(8)], axis=0),
        jnp.concatenate([bt_ref[q * 128 : q * 128 + 16] for q in range(4)], axis=0),
        bt_ref[pl.ds(0, FLAT, stride=8)],
    )
    upper = (
        jnp.concatenate([bt_ref[392 + yy * 16 : 400 + yy * 16] for yy in range(8)], axis=0),
        jnp.concatenate([bt_ref[q * 128 + 112 : q * 128 + 128] for q in range(4)], axis=0),
        bt_ref[pl.ds(7, FLAT, stride=8)],
    )
    pieces = [
        jnp.where(upper_side(axis, odd), upper[AXES.index(axis)], lower[AXES.index(axis)])
        for axis, odd in SLOTS
    ]
    faces_t = jnp.concatenate(pieces, axis=0)
    ft = faces_t[:, :ROWS]
    ft_ref[...] = ft
    df_ref[:, :BODY] = -0.5 * faces_t.T[:ROWS]
    df_ref[:, BODY : BODY + ROWS] = diagonal
    df_ref[:, BODY + ROWS :] = jnp.zeros((ROWS, WIDTH - BODY - ROWS), jnp.float32)
    send_traces(ft, vectors_ref[...], sent, held_ref, sems)


def step_kernel(first, last, scal_ref, df_ref, ft_ref, now_ref, prior_ref, *refs):
    swap_refs, cube_ref, out_ref, rest = refs[:3], refs[3], refs[4], refs[5:]
    now = now_ref[...]
    at = place()
    halos = [ref[...] for ref in swap_refs] + [cube_ref[at ^ flip] for flip in FLIPS]
    first_half = halos[:4]
    second_half = halos[4:] + [now, jnp.zeros((WIDTH - BODY - ROWS, COLS), jnp.float32)]
    result = dot3(
        split(df_ref[:, : WIDTH // 2]), split(jnp.concatenate(first_half, axis=0))
    ) + dot3(split(df_ref[:, WIDTH // 2 :]), split(jnp.concatenate(second_half, axis=0)))
    centre, half_width = scal_ref[0], scal_ref[1]
    following = (result - centre * now) / half_width
    if not first:
        following = 2.0 * following - prior_ref[...]
    out_ref[...] = following
    if not last:
        send_traces(ft_ref[...], following, rest[:4], rest[4], rest[5])


def vmem():
    return pl.BlockSpec(memory_space=pltpu.VMEM)


def smem():
    return pl.BlockSpec(memory_space=pltpu.SMEM)


def of(*shape):
    return jax.ShapeDtypeStruct(shape, jnp.float32)


def call(kernel, name, out_shape, in_specs, out_specs, scratch=()):
    return pl.pallas_call(
        kernel,
        out_shape=out_shape,
        in_specs=in_specs,
        out_specs=out_specs,
        scratch_shapes=list(scratch),
        compiler_params=pltpu.CompilerParams(vmem_limit_bytes=GRANT),
        name=name,
    )


def per_device(orbitals, potential, coefficients):
    f32 = jnp.float32
    nx = lax.axis_size("gx")
    plane = lax.axis_size("gy") * lax.axis_size("gz")
    tile, peak = call(
        tile_kernel, "tile", (of(8, 128), of(nx, 1, 128)), [vmem()], (vmem(), vmem())
    )(potential)
    below = shifted(tile, "gx", 1)
    peaks = lax.all_to_all(peak, "gx", 0, 0)
    block = call(block_kernel, "block", of(plane, 8, 128), [vmem()] * 3, vmem())(tile, below, peaks)
    tiles = lax.all_to_all(block, ("gy", "gz"), 0, 0)
    start = coefficients.reshape(ROWS, COLS)
    sent_shapes = (of(FLAT, COLS),) * 3 + (of(CUBE, FLAT, COLS),)
    sent_specs = (vmem(),) * 3 + (pl.BlockSpec(memory_space=pltpu.HBM),)
    staging = [pltpu.VMEM((3, FLAT, COLS), f32), pltpu.SemaphoreType.DMA((3,))]
    df, ft, scal, *sent = call(
        basis_kernel,
        "basis",
        (of(ROWS, WIDTH), of(BODY, ROWS), of(2)) + sent_shapes,
        [vmem()] * 3,
        (vmem(), vmem(), smem()) + sent_specs,
        [pltpu.VMEM((10, 8, 256), f32), pltpu.VMEM((ROWS, WIDTH), f32), pltpu.VMEM((WIDTH, 128), f32)]
        + staging,
    )(tiles, orbitals.reshape(ROWS, -1), start)

    groups = cubes()
    prior, now = start, start
    for step in range(DG_STEPS):
        halos = [swapped(trace, *pairing) for trace, pairing in zip(sent, SWAPS)]
        halos.append(lax.all_to_all(sent[3], AXES, 0, 0, axis_index_groups=groups))
        last = step == DG_STEPS - 1

        def body(*refs, step=step, last=last):
            step_kernel(step == 0, last, *refs)

        following, *sent = call(
            body,
            f"step{step}",
            (of(ROWS, COLS),) + (() if last else sent_shapes),
            [smem()] + [vmem()] * 8,
            (vmem(),) + (() if last else sent_specs),
            () if last else staging,
        )(scal, df, ft, now, prior, *halos)
        prior, now = now, following
    return now.reshape(coefficients.shape)


def solution(mesh):
    placed = (P("gx", "gy", "gz", None, None), P("gx", "gy", "gz"), P("gx", "gy", "gz", None, None))
    return jax.shard_map(
        per_device,
        mesh=mesh,
        in_specs=placed,
        out_specs=P("gx", "gy", "gz", None, None),
        check_vma=False,
    )
```

```python
import jax
import jax.numpy as jnp
from jax import lax
from jax.experimental import pallas as pl
from jax.experimental.pallas import tpu as pltpu
from jax.sharding import PartitionSpec as P

NEWTON = 6
DG_STEPS = 3
SHIFT = 3.0
ROWS = 96
EDGE = 8
FLAT = EDGE * EDGE
COLS = 256
FACES = 6
CUBE = 8
GRANT = 16 << 20
BODY = FACES * FLAT
WIDTH = 512
cutoff = 1.0


def shifted(shard, axis, by):
    count = lax.axis_size(axis)
    return lax.ppermute(shard, axis, [(i, (i + by) % count) for i in range(count)])


def split(value):
    high = value.astype(jnp.bfloat16)
    low = (value - high.astype(jnp.float32)).astype(jnp.bfloat16)
    return high, low


def dot3(left, right, dims=(((1,), (0,)), ((), ()))):
    lh, ll = left
    rh, rl = right
    rows = lh.shape[0]

    def one(a, b):
        return lax.dot_general(a, b, dims, preferred_element_type=jnp.float32)

    both = one(jnp.concatenate([lh, ll], axis=0), rh)
    return both[:rows] + (both[rows:] + one(lh, rl))


def exact(left, right, dims=(((1,), (0,)), ((), ()))):
    return lax.dot_general(
        left, right, dims, precision=lax.Precision.HIGHEST, preferred_element_type=jnp.float32
    )


def product(left, right):
    return dot3(split(left), split(right))


def lane_roll(value, by):
    return pltpu.roll(value, by % value.shape[-1], axis=value.ndim - 1)


def lanes(shape):
    return lax.broadcasted_iota(jnp.int32, shape, len(shape) - 1)


SWAPS = (("gz", 1), ("gx", 1), ("gy", 0))
CUBE_PAIRS = (("gx", 0), ("gy", 1), ("gz", 0))
SLOTS = SWAPS + CUBE_PAIRS
AXES = ("gx", "gy", "gz")
FLIPS = (4, 2, 1)


def upper_side(axis, odd):
    return lax.rem(lax.axis_index(axis), 2) == odd


def swapped(shard, axis, odd):
    count = lax.axis_size(axis)
    pairs = [((2 * i + odd) % count, (2 * i + 1 + odd) % count) for i in range(count // 2)]
    return lax.ppermute(shard, axis, pairs + [(b, a) for a, b in pairs])


def place():
    return sum(
        flip * lax.rem(lax.axis_index(axis) + odd, 2) for flip, (axis, odd) in zip(FLIPS, CUBE_PAIRS)
    )


def cubes():
    sizes = [lax.axis_size(axis) for axis in AXES]
    groups = []
    for base in ((i, j, k) for i in range(sizes[0] // 2) for j in range(sizes[1] // 2) for k in range(sizes[2] // 2)):
        group = []
        for spot in range(CUBE):
            x, y, z = [
                (2 * base[n] + CUBE_PAIRS[n][1] + (spot // FLIPS[n]) % 2) % sizes[n] for n in range(3)
            ]
            group.append((x * sizes[1] + y) * sizes[2] + z)
        groups.append(group)
    return groups


def tile_kernel(potential_ref, out_ref):
    lane = lanes((8, 128))
    tile = jnp.full((8, 128), jnp.max(potential_ref[...]))
    for y in range(8):
        row = jnp.concatenate([potential_ref[:, y, :], jnp.zeros((8, 120), jnp.float32)], axis=1)
        if y:
            row = lane_roll(row, 16 * y)
        tile = jnp.where((lane >= 16 * y) & (lane < 16 * y + 8), row, tile)
    out_ref[...] = jnp.broadcast_to(tile, out_ref.shape)


def tiles_kernel(tiles_ref, peak_ref, wide_ref):
    ny = lax.axis_size("gy")
    nz = lax.axis_size("gz")
    gy = lax.axis_index("gy")
    gz = lax.axis_index("gz")
    py = lax.rem(gy + ny - 1, ny)
    pz = lax.rem(gz + nz - 1, nz)
    near = lanes((8, 128)) % 16 < 8
    peak_ref[...] = jnp.broadcast_to(jnp.max(tiles_ref[...]), peak_ref.shape)
    for half, row in enumerate((py, gy)):
        low = tiles_ref[row * nz + pz]
        high = tiles_ref[row * nz + gz]
        wide_ref[:, half * 128 : (half + 1) * 128] = jnp.where(near, low, lane_roll(high, 8))


def filter_kernel(wide_ref, below_ref, orbitals_ref, u0_ref, u1_ref, u2_ref, own_ref, w_ref):
    first_half = lanes((8, 128)) % 16 < 8

    def packed(even, odd):
        return jnp.where(first_half, lane_roll(even, -68)[:, :128], lane_roll(odd, -60)[:, :128])

    planes = {}
    for plane in range(3, 13):
        row = below_ref[plane : plane + 1] if plane < 8 else wide_ref[plane - 8 : plane - 7]
        planes[plane] = jnp.broadcast_to(row, (8, 256)) + (3.0 - SHIFT)
        w_ref[plane - 3] = planes[plane]
    for q in range(4):
        own_ref[:, q * 128 : (q + 1) * 128] = packed(planes[4 + 2 * q], planes[5 + 2 * q])

    def around(value):
        return (
            lane_roll(value, 1) + lane_roll(value, -1) + lane_roll(value, 16) + lane_roll(value, -16)
        )

    def filter_rows(step, carry):
        rows = pl.ds(pl.multiple_of(step * 8, 8), 8)
        start = {p: orbitals_ref[rows, p * 256 : (p + 1) * 256] for p in range(2, 14)}
        once = {}
        for p in range(3, 13):
            total = around(start[p]) + (start[p - 1] + start[p + 1])
            once[p] = w_ref[p - 3] * start[p] - 0.5 * total
        twice = {}
        for p in range(4, 12):
            total = around(once[p]) + (once[p - 1] + once[p + 1])
            twice[p] = w_ref[p - 3] * once[p] - 0.5 * total
        for q in range(4):
            at = slice(q * 128, (q + 1) * 128)
            u0_ref[rows, at] = packed(start[4 + 2 * q], start[5 + 2 * q])
            u1_ref[rows, at] = packed(once[4 + 2 * q], once[5 + 2 * q])
            u2_ref[rows, at] = packed(twice[4 + 2 * q], twice[5 + 2 * q])
        return carry

    lax.fori_loop(0, ROWS // 8, filter_rows, 0)


def send_traces(ft, value, sent, held_ref, sems):
    right = split(value)
    half = BODY // 2
    traces = dot3(split(ft[half:]), right)
    at = place()
    copies = []
    for n, flip in enumerate(FLIPS):
        held_ref[n] = traces[n * FLAT : (n + 1) * FLAT]
        copies.append(pltpu.make_async_copy(held_ref.at[n], sent[3].at[at ^ flip], sems.at[n]))
        copies[-1].start()
    traces = dot3(split(ft[:half]), right)
    for slot in range(3):
        sent[slot][...] = traces[slot * FLAT : (slot + 1) * FLAT]
    for copy in copies:
        copy.wait()


def basis_kernel(peaks_ref, u0_ref, u1_ref, u2_ref, own_ref, vectors_ref,
                 df_ref, ft_ref, scal_ref, *refs):
    sent, (bt_ref, held_ref, sems) = refs[:-3], refs[-3:]
    top = 6.0 + jnp.max(peaks_ref[...])
    centre = (top + cutoff) / 2.0
    half_width = (top - cutoff) / 2.0
    scal_ref[0] = centre
    scal_ref[1] = half_width
    moved = SHIFT - centre
    start = u0_ref[...]
    square = u2_ref[...] + (2.0 * moved) * u1_ref[...] + (moved * moved) * start
    restricted = square * (2.0 / (half_width * half_width)) - start
    halves = split(restricted)
    intersection = dot3(halves, halves, (((1,), (1,)), ((), ())))
    sigma = jnp.sqrt(jnp.sum(intersection * intersection))
    identity = (
        lax.broadcasted_iota(jnp.int32, (ROWS, ROWS), 0) == lanes((ROWS, ROWS))
    ).astype(jnp.float32)
    current = intersection / sigma
    factor = 1.5 * identity - 0.5 * current
    current = product(current, factor)
    root = factor
    for step in range(NEWTON - 1):
        factor = 1.5 * identity - 0.5 * product(root, current)
        if step < NEWTON - 2:
            current = product(current, factor)
        root = product(factor, root)
    root = root / jnp.sqrt(sigma)
    basis = dot3(split(root), halves)

    own = own_ref[:1] + SHIFT
    cell = lanes((ROWS, WIDTH))
    z = cell % 8
    y = cell // 16 % 8
    x = cell // 128 * 2 + cell // 8 % 2
    odd = x % 2 == 1

    def gate(ok, value):
        return jnp.where(ok, value, 0.0)

    total = gate(z > 0, lane_roll(basis, 1)) + gate(z < 7, lane_roll(basis, -1))
    total = total + gate(y > 0, lane_roll(basis, 16)) + gate(y < 7, lane_roll(basis, -16))
    total = total + jnp.where(odd, lane_roll(basis, 8), lane_roll(basis, -8))
    total = total + gate(
        (x > 0) & (x < 7), jnp.where(odd, lane_roll(basis, -120), lane_roll(basis, 120))
    )
    applied = own * basis - 0.5 * total
    diagonal = dot3(split(basis), split(applied), (((1,), (1,)), ((), ())))

    bt_ref[...] = jnp.concatenate([basis, jnp.zeros((128 - ROWS, WIDTH), jnp.float32)], axis=0).T
    lower = (
        jnp.concatenate([bt_ref[yy * 16 : yy * 16 + 8] for yy in range(8)], axis=0),
        jnp.concatenate([bt_ref[q * 128 : q * 128 + 16] for q in range(4)], axis=0),
        bt_ref[pl.ds(0, FLAT, stride=8)],
    )
    upper = (
        jnp.concatenate([bt_ref[392 + yy * 16 : 400 + yy * 16] for yy in range(8)], axis=0),
        jnp.concatenate([bt_ref[q * 128 + 112 : q * 128 + 128] for q in range(4)], axis=0),
        bt_ref[pl.ds(7, FLAT, stride=8)],
    )
    pieces = [
        jnp.where(upper_side(axis, odd), upper[AXES.index(axis)], lower[AXES.index(axis)])
        for axis, odd in SLOTS
    ]
    faces_t = jnp.concatenate(pieces, axis=0)
    ft = faces_t[:, :ROWS]
    ft_ref[...] = ft
    df_ref[:, :BODY] = -0.5 * faces_t.T[:ROWS]
    df_ref[:, BODY : BODY + ROWS] = diagonal
    df_ref[:, BODY + ROWS :] = jnp.zeros((ROWS, WIDTH - BODY - ROWS), jnp.float32)
    send_traces(ft, vectors_ref[...], sent, held_ref, sems)


def step_kernel(first, last, scal_ref, df_ref, ft_ref, now_ref, prior_ref, *refs):
    swap_refs, cube_ref, out_ref, rest = refs[:3], refs[3], refs[4], refs[5:]
    now = now_ref[...]
    at = place()
    halos = [ref[...] for ref in swap_refs] + [cube_ref[at ^ flip] for flip in FLIPS]
    first_half = halos[:4]
    second_half = halos[4:] + [now, jnp.zeros((WIDTH - BODY - ROWS, COLS), jnp.float32)]
    result = dot3(
        split(df_ref[:, : WIDTH // 2]), split(jnp.concatenate(first_half, axis=0))
    ) + dot3(split(df_ref[:, WIDTH // 2 :]), split(jnp.concatenate(second_half, axis=0)))
    centre, half_width = scal_ref[0], scal_ref[1]
    following = (result - centre * now) / half_width
    if not first:
        following = 2.0 * following - prior_ref[...]
    out_ref[...] = following
    if not last:
        send_traces(ft_ref[...], following, rest[:4], rest[4], rest[5])


def vmem():
    return pl.BlockSpec(memory_space=pltpu.VMEM)


def smem():
    return pl.BlockSpec(memory_space=pltpu.SMEM)


def of(*shape):
    return jax.ShapeDtypeStruct(shape, jnp.float32)


def call(kernel, name, out_shape, in_specs, out_specs, scratch=()):
    return pl.pallas_call(
        kernel,
        out_shape=out_shape,
        in_specs=in_specs,
        out_specs=out_specs,
        scratch_shapes=list(scratch),
        compiler_params=pltpu.CompilerParams(vmem_limit_bytes=GRANT),
        name=name,
    )


def per_device(orbitals, potential, coefficients):
    f32 = jnp.float32
    nx = lax.axis_size("gx")
    plane = lax.axis_size("gy") * lax.axis_size("gz")
    tile = call(tile_kernel, "tile", of(plane, 8, 128), [vmem()], vmem())(potential)
    tiles = lax.all_to_all(tile, ("gy", "gz"), 0, 0)
    peak, wide = call(
        tiles_kernel, "tiles", (of(nx, 1, 128), of(8, 256)), [vmem()], (vmem(), vmem())
    )(tiles)
    peaks = lax.all_to_all(peak, "gx", 0, 0)
    below = shifted(wide, "gx", 1)
    powers = call(
        filter_kernel,
        "powers",
        (of(ROWS, WIDTH),) * 3 + (of(8, WIDTH),),
        [vmem()] * 3,
        (vmem(),) * 4,
        [pltpu.VMEM((10, 8, 256), f32)],
    )(wide, below, orbitals.reshape(ROWS, -1))
    start = coefficients.reshape(ROWS, COLS)
    sent_shapes = (of(FLAT, COLS),) * 3 + (of(CUBE, FLAT, COLS),)
    sent_specs = (vmem(),) * 3 + (pl.BlockSpec(memory_space=pltpu.HBM),)
    staging = [pltpu.VMEM((3, FLAT, COLS), f32), pltpu.SemaphoreType.DMA((3,))]
    df, ft, scal, *sent = call(
        basis_kernel,
        "basis",
        (of(ROWS, WIDTH), of(BODY, ROWS), of(2)) + sent_shapes,
        [vmem()] * 6,
        (vmem(), vmem(), smem()) + sent_specs,
        [pltpu.VMEM((WIDTH, 128), f32)] + staging,
    )(peaks, *powers, start)

    groups = cubes()
    prior, now = start, start
    for step in range(DG_STEPS):
        halos = [swapped(trace, *pairing) for trace, pairing in zip(sent, SWAPS)]
        halos.append(lax.all_to_all(sent[3], AXES, 0, 0, axis_index_groups=groups))
        last = step == DG_STEPS - 1

        def body(*refs, step=step, last=last):
            step_kernel(step == 0, last, *refs)

        following, *sent = call(
            body,
            f"step{step}",
            (of(ROWS, COLS),) + (() if last else sent_shapes),
            [smem()] + [vmem()] * 8,
            (vmem(),) + (() if last else sent_specs),
            () if last else staging,
        )(scal, df, ft, now, prior, *halos)
        prior, now = now, following
    return now.reshape(coefficients.shape)


def solution(mesh):
    placed = (P("gx", "gy", "gz", None, None), P("gx", "gy", "gz"), P("gx", "gy", "gz", None, None))
    return jax.shard_map(
        per_device,
        mesh=mesh,
        in_specs=placed,
        out_specs=P("gx", "gy", "gz", None, None),
        check_vma=False,
    )
```

```python
import jax
import jax.numpy as jnp
from jax import lax
from jax.experimental import pallas as pl
from jax.experimental.pallas import tpu as pltpu
from jax.sharding import PartitionSpec as P

NEWTON = 6
DG_STEPS = 3
SHIFT = 3.0
ROWS = 96
EDGE = 8
FLAT = EDGE * EDGE
COLS = 256
FACES = 6
CUBE = 8
GRANT = 16 << 20
BODY = FACES * FLAT
WIDTH = 512
cutoff = 1.0


def shifted(shard, axis, by):
    count = lax.axis_size(axis)
    return lax.ppermute(shard, axis, [(i, (i + by) % count) for i in range(count)])


def split(value):
    high = value.astype(jnp.bfloat16)
    low = (value - high.astype(jnp.float32)).astype(jnp.bfloat16)
    return high, low


def dot3(left, right, dims=(((1,), (0,)), ((), ()))):
    lh, ll = left
    rh, rl = right
    rows = lh.shape[0]

    def one(a, b):
        return lax.dot_general(a, b, dims, preferred_element_type=jnp.float32)

    both = one(jnp.concatenate([lh, ll], axis=0), rh)
    return both[:rows] + (both[rows:] + one(lh, rl))


def exact(left, right, dims=(((1,), (0,)), ((), ()))):
    return lax.dot_general(
        left, right, dims, precision=lax.Precision.HIGHEST, preferred_element_type=jnp.float32
    )


def product(left, right):
    return dot3(split(left), split(right))


def lane_roll(value, by):
    return pltpu.roll(value, by % value.shape[-1], axis=value.ndim - 1)


def lanes(shape):
    return lax.broadcasted_iota(jnp.int32, shape, len(shape) - 1)


SWAPS = (("gz", 1), ("gx", 1), ("gy", 0))
CUBE_PAIRS = (("gx", 0), ("gy", 1), ("gz", 0))
SLOTS = SWAPS + CUBE_PAIRS
AXES = ("gx", "gy", "gz")
FLIPS = (4, 2, 1)


def upper_side(axis, odd):
    return lax.rem(lax.axis_index(axis), 2) == odd


def swapped(shard, axis, odd):
    count = lax.axis_size(axis)
    pairs = [((2 * i + odd) % count, (2 * i + 1 + odd) % count) for i in range(count // 2)]
    return lax.ppermute(shard, axis, pairs + [(b, a) for a, b in pairs])


def place():
    return sum(
        flip * lax.rem(lax.axis_index(axis) + odd, 2) for flip, (axis, odd) in zip(FLIPS, CUBE_PAIRS)
    )


def cubes():
    sizes = [lax.axis_size(axis) for axis in AXES]
    groups = []
    for base in ((i, j, k) for i in range(sizes[0] // 2) for j in range(sizes[1] // 2) for k in range(sizes[2] // 2)):
        group = []
        for spot in range(CUBE):
            x, y, z = [
                (2 * base[n] + CUBE_PAIRS[n][1] + (spot // FLIPS[n]) % 2) % sizes[n] for n in range(3)
            ]
            group.append((x * sizes[1] + y) * sizes[2] + z)
        groups.append(group)
    return groups


def tile_kernel(potential_ref, out_ref):
    lane = lanes((8, 128))
    tile = jnp.full((8, 128), jnp.max(potential_ref[...]))
    for y in range(8):
        row = jnp.concatenate([potential_ref[:, y, :], jnp.zeros((8, 120), jnp.float32)], axis=1)
        if y:
            row = lane_roll(row, 16 * y)
        tile = jnp.where((lane >= 16 * y) & (lane < 16 * y + 8), row, tile)
    out_ref[...] = jnp.broadcast_to(tile, out_ref.shape)


def tiles_kernel(tiles_ref, peak_ref, wide_ref):
    ny = lax.axis_size("gy")
    nz = lax.axis_size("gz")
    gy = lax.axis_index("gy")
    gz = lax.axis_index("gz")
    py = lax.rem(gy + ny - 1, ny)
    pz = lax.rem(gz + nz - 1, nz)
    near = lanes((8, 128)) % 16 < 8
    peak_ref[...] = jnp.broadcast_to(jnp.max(tiles_ref[...]), peak_ref.shape)
    for half, row in enumerate((py, gy)):
        low = tiles_ref[row * nz + pz]
        high = tiles_ref[row * nz + gz]
        wide_ref[:, half * 128 : (half + 1) * 128] = jnp.where(near, low, lane_roll(high, 8))


def filter_kernel(wide_ref, below_ref, orbitals_ref, u0_ref, u1_ref, u2_ref, own_ref, w_ref):
    first_half = lanes((8, 128)) % 16 < 8

    def packed(even, odd):
        return jnp.where(first_half, lane_roll(even, -68)[:, :128], lane_roll(odd, -60)[:, :128])

    planes = {}
    for plane in range(3, 13):
        row = below_ref[plane : plane + 1] if plane < 8 else wide_ref[plane - 8 : plane - 7]
        planes[plane] = jnp.broadcast_to(row, (8, 256)) + (3.0 - SHIFT)
        w_ref[plane - 3] = planes[plane]
    for q in range(4):
        own_ref[:, q * 128 : (q + 1) * 128] = packed(planes[4 + 2 * q], planes[5 + 2 * q])

    def around(value):
        return (
            lane_roll(value, 1) + lane_roll(value, -1) + lane_roll(value, 16) + lane_roll(value, -16)
        )

    def filter_rows(step, carry):
        rows = pl.ds(pl.multiple_of(step * 8, 8), 8)
        start = {p: orbitals_ref[rows, p * 256 : (p + 1) * 256] for p in range(2, 14)}
        once = {}
        for p in range(3, 13):
            total = around(start[p]) + (start[p - 1] + start[p + 1])
            once[p] = w_ref[p - 3] * start[p] - 0.5 * total
        twice = {}
        for p in range(4, 12):
            total = around(once[p]) + (once[p - 1] + once[p + 1])
            twice[p] = w_ref[p - 3] * once[p] - 0.5 * total
        for q in range(4):
            at = slice(q * 128, (q + 1) * 128)
            u0_ref[rows, at] = packed(start[4 + 2 * q], start[5 + 2 * q])
            u1_ref[rows, at] = packed(once[4 + 2 * q], once[5 + 2 * q])
            u2_ref[rows, at] = packed(twice[4 + 2 * q], twice[5 + 2 * q])
        return carry

    lax.fori_loop(0, ROWS // 8, filter_rows, 0)


def send_traces(ft, value, sent, held_ref, sems):
    right = split(value)
    half = BODY // 2
    traces = dot3(split(ft[half:]), right)
    at = place()
    copies = []
    for n, flip in enumerate(FLIPS):
        held_ref[n] = traces[n * FLAT : (n + 1) * FLAT]
        copies.append(pltpu.make_async_copy(held_ref.at[n], sent[3].at[at ^ flip], sems.at[n]))
        copies[-1].start()
    traces = dot3(split(ft[:half]), right)
    for slot in range(3):
        sent[slot][...] = traces[slot * FLAT : (slot + 1) * FLAT]
    for copy in copies:
        copy.wait()


def basis_kernel(peaks_ref, u0_ref, u1_ref, u2_ref, vectors_ref,
                 basis_ref, ft_ref, scal_ref, *refs):
    sent, (bt_ref, held_ref, sems) = refs[:-3], refs[-3:]
    top = 6.0 + jnp.max(peaks_ref[...])
    centre = (top + cutoff) / 2.0
    half_width = (top - cutoff) / 2.0
    scal_ref[0] = centre
    scal_ref[1] = half_width
    moved = SHIFT - centre
    start = u0_ref[...]
    square = u2_ref[...] + (2.0 * moved) * u1_ref[...] + (moved * moved) * start
    restricted = square * (2.0 / (half_width * half_width)) - start
    halves = split(restricted)
    intersection = dot3(halves, halves, (((1,), (1,)), ((), ())))
    sigma = jnp.sqrt(jnp.sum(intersection * intersection))
    identity = (
        lax.broadcasted_iota(jnp.int32, (ROWS, ROWS), 0) == lanes((ROWS, ROWS))
    ).astype(jnp.float32)
    current = intersection / sigma
    factor = 1.5 * identity - 0.5 * current
    current = product(current, factor)
    root = factor
    for step in range(NEWTON - 1):
        factor = 1.5 * identity - 0.5 * product(root, current)
        if step < NEWTON - 2:
            current = product(current, factor)
        root = product(factor, root)
    root = root / jnp.sqrt(sigma)
    basis = dot3(split(root), halves)

    basis_ref[...] = basis
    bt_ref[...] = jnp.concatenate([basis, jnp.zeros((128 - ROWS, WIDTH), jnp.float32)], axis=0).T
    lower = (
        jnp.concatenate([bt_ref[yy * 16 : yy * 16 + 8] for yy in range(8)], axis=0),
        jnp.concatenate([bt_ref[q * 128 : q * 128 + 16] for q in range(4)], axis=0),
        bt_ref[pl.ds(0, FLAT, stride=8)],
    )
    upper = (
        jnp.concatenate([bt_ref[392 + yy * 16 : 400 + yy * 16] for yy in range(8)], axis=0),
        jnp.concatenate([bt_ref[q * 128 + 112 : q * 128 + 128] for q in range(4)], axis=0),
        bt_ref[pl.ds(7, FLAT, stride=8)],
    )
    pieces = [
        jnp.where(upper_side(axis, odd), upper[AXES.index(axis)], lower[AXES.index(axis)])
        for axis, odd in SLOTS
    ]
    faces_t = jnp.concatenate(pieces, axis=0)
    ft = faces_t[:, :ROWS]
    ft_ref[...] = ft
    send_traces(ft, vectors_ref[...], sent, held_ref, sems)


def coupling_kernel(basis_ref, own_ref, ft_ref, df_ref):
    basis = basis_ref[...]
    own = own_ref[:1] + SHIFT
    cell = lanes((ROWS, WIDTH))
    z = cell % 8
    y = cell // 16 % 8
    x = cell // 128 * 2 + cell // 8 % 2
    odd = x % 2 == 1

    def gate(ok, value):
        return jnp.where(ok, value, 0.0)

    total = gate(z > 0, lane_roll(basis, 1)) + gate(z < 7, lane_roll(basis, -1))
    total = total + gate(y > 0, lane_roll(basis, 16)) + gate(y < 7, lane_roll(basis, -16))
    total = total + jnp.where(odd, lane_roll(basis, 8), lane_roll(basis, -8))
    total = total + gate(
        (x > 0) & (x < 7), jnp.where(odd, lane_roll(basis, -120), lane_roll(basis, 120))
    )
    applied = own * basis - 0.5 * total
    diagonal = dot3(split(basis), split(applied), (((1,), (1,)), ((), ())))
    df_ref[:, :BODY] = -0.5 * ft_ref[...].T
    df_ref[:, BODY : BODY + ROWS] = diagonal
    df_ref[:, BODY + ROWS :] = jnp.zeros((ROWS, WIDTH - BODY - ROWS), jnp.float32)


def step_kernel(first, last, scal_ref, df_ref, ft_ref, now_ref, prior_ref, *refs):
    swap_refs, cube_ref, out_ref, rest = refs[:3], refs[3], refs[4], refs[5:]
    now = now_ref[...]
    at = place()
    halos = [ref[...] for ref in swap_refs] + [cube_ref[at ^ flip] for flip in FLIPS]
    first_half = halos[:4]
    second_half = halos[4:] + [now, jnp.zeros((WIDTH - BODY - ROWS, COLS), jnp.float32)]
    result = dot3(
        split(df_ref[:, : WIDTH // 2]), split(jnp.concatenate(first_half, axis=0))
    ) + dot3(split(df_ref[:, WIDTH // 2 :]), split(jnp.concatenate(second_half, axis=0)))
    centre, half_width = scal_ref[0], scal_ref[1]
    following = (result - centre * now) / half_width
    if not first:
        following = 2.0 * following - prior_ref[...]
    out_ref[...] = following
    if not last:
        send_traces(ft_ref[...], following, rest[:4], rest[4], rest[5])


def vmem():
    return pl.BlockSpec(memory_space=pltpu.VMEM)


def smem():
    return pl.BlockSpec(memory_space=pltpu.SMEM)


def of(*shape):
    return jax.ShapeDtypeStruct(shape, jnp.float32)


def call(kernel, name, out_shape, in_specs, out_specs, scratch=()):
    return pl.pallas_call(
        kernel,
        out_shape=out_shape,
        in_specs=in_specs,
        out_specs=out_specs,
        scratch_shapes=list(scratch),
        compiler_params=pltpu.CompilerParams(vmem_limit_bytes=GRANT),
        name=name,
    )


def per_device(orbitals, potential, coefficients):
    f32 = jnp.float32
    nx = lax.axis_size("gx")
    plane = lax.axis_size("gy") * lax.axis_size("gz")
    tile = call(tile_kernel, "tile", of(plane, 8, 128), [vmem()], vmem())(potential)
    tiles = lax.all_to_all(tile, ("gy", "gz"), 0, 0)
    peak, wide = call(
        tiles_kernel, "tiles", (of(nx, 1, 128), of(8, 256)), [vmem()], (vmem(), vmem())
    )(tiles)
    peaks = lax.all_to_all(peak, "gx", 0, 0)
    below = shifted(wide, "gx", 1)
    *powers, own = call(
        filter_kernel,
        "powers",
        (of(ROWS, WIDTH),) * 3 + (of(8, WIDTH),),
        [vmem()] * 3,
        (vmem(),) * 4,
        [pltpu.VMEM((10, 8, 256), f32)],
    )(wide, below, orbitals.reshape(ROWS, -1))
    start = coefficients.reshape(ROWS, COLS)
    sent_shapes = (of(FLAT, COLS),) * 3 + (of(CUBE, FLAT, COLS),)
    sent_specs = (vmem(),) * 3 + (pl.BlockSpec(memory_space=pltpu.HBM),)
    staging = [pltpu.VMEM((3, FLAT, COLS), f32), pltpu.SemaphoreType.DMA((3,))]
    basis, ft, scal, *sent = call(
        basis_kernel,
        "basis",
        (of(ROWS, WIDTH), of(BODY, ROWS), of(2)) + sent_shapes,
        [vmem()] * 5,
        (vmem(), vmem(), smem()) + sent_specs,
        [pltpu.VMEM((WIDTH, 128), f32)] + staging,
    )(peaks, *powers, start)
    df = call(coupling_kernel, "coupling", of(ROWS, WIDTH), [vmem()] * 3, vmem())(basis, own, ft)

    groups = cubes()
    prior, now = start, start
    for step in range(DG_STEPS):
        halos = [swapped(trace, *pairing) for trace, pairing in zip(sent, SWAPS)]
        halos.append(lax.all_to_all(sent[3], AXES, 0, 0, axis_index_groups=groups))
        last = step == DG_STEPS - 1

        def body(*refs, step=step, last=last):
            step_kernel(step == 0, last, *refs)

        following, *sent = call(
            body,
            f"step{step}",
            (of(ROWS, COLS),) + (() if last else sent_shapes),
            [smem()] + [vmem()] * 8,
            (vmem(),) + (() if last else sent_specs),
            () if last else staging,
        )(scal, df, ft, now, prior, *halos)
        prior, now = now, following
    return now.reshape(coefficients.shape)


def solution(mesh):
    placed = (P("gx", "gy", "gz", None, None), P("gx", "gy", "gz"), P("gx", "gy", "gz", None, None))
    return jax.shard_map(
        per_device,
        mesh=mesh,
        in_specs=placed,
        out_specs=P("gx", "gy", "gz", None, None),
        check_vma=False,
    )
```

```python
import jax
import jax.numpy as jnp
from jax import lax
from jax.experimental import pallas as pl
from jax.experimental.pallas import tpu as pltpu
from jax.sharding import PartitionSpec as P

NEWTON = 6
DG_STEPS = 3
SHIFT = 3.0
ROWS = 96
EDGE = 8
FLAT = EDGE * EDGE
COLS = 256
FACES = 6
CUBE = 8
GRANT = 16 << 20
BODY = FACES * FLAT
WIDTH = 512
cutoff = 1.0


def shifted(shard, axis, by):
    count = lax.axis_size(axis)
    return lax.ppermute(shard, axis, [(i, (i + by) % count) for i in range(count)])


def split(value):
    high = value.astype(jnp.bfloat16)
    low = (value - high.astype(jnp.float32)).astype(jnp.bfloat16)
    return high, low


def dot3(left, right, dims=(((1,), (0,)), ((), ()))):
    lh, ll = left
    rh, rl = right
    rows = lh.shape[0]

    def one(a, b):
        return lax.dot_general(a, b, dims, preferred_element_type=jnp.float32)

    both = one(jnp.concatenate([lh, ll], axis=0), rh)
    return both[:rows] + (both[rows:] + one(lh, rl))


def exact(left, right, dims=(((1,), (0,)), ((), ()))):
    return lax.dot_general(
        left, right, dims, precision=lax.Precision.HIGHEST, preferred_element_type=jnp.float32
    )


def product(left, right):
    return dot3(split(left), split(right))


def lane_roll(value, by):
    return pltpu.roll(value, by % value.shape[-1], axis=value.ndim - 1)


def lanes(shape):
    return lax.broadcasted_iota(jnp.int32, shape, len(shape) - 1)


SWAPS = (("gz", 1), ("gx", 1), ("gy", 0))
CUBE_PAIRS = (("gx", 0), ("gy", 1), ("gz", 0))
SLOTS = SWAPS + CUBE_PAIRS
AXES = ("gx", "gy", "gz")
FLIPS = (4, 2, 1)


def upper_side(axis, odd):
    return lax.rem(lax.axis_index(axis), 2) == odd


def swapped(shard, axis, odd):
    count = lax.axis_size(axis)
    pairs = [((2 * i + odd) % count, (2 * i + 1 + odd) % count) for i in range(count // 2)]
    return lax.ppermute(shard, axis, pairs + [(b, a) for a, b in pairs])


def place():
    return sum(
        flip * lax.rem(lax.axis_index(axis) + odd, 2) for flip, (axis, odd) in zip(FLIPS, CUBE_PAIRS)
    )


def cubes():
    sizes = [lax.axis_size(axis) for axis in AXES]
    groups = []
    for base in ((i, j, k) for i in range(sizes[0] // 2) for j in range(sizes[1] // 2) for k in range(sizes[2] // 2)):
        group = []
        for spot in range(CUBE):
            x, y, z = [
                (2 * base[n] + CUBE_PAIRS[n][1] + (spot // FLIPS[n]) % 2) % sizes[n] for n in range(3)
            ]
            group.append((x * sizes[1] + y) * sizes[2] + z)
        groups.append(group)
    return groups


def tile_kernel(potential_ref, out_ref):
    lane = lanes((8, 128))
    tile = jnp.full((8, 128), jnp.max(potential_ref[...]))
    for y in range(8):
        row = jnp.concatenate([potential_ref[:, y, :], jnp.zeros((8, 120), jnp.float32)], axis=1)
        if y:
            row = lane_roll(row, 16 * y)
        tile = jnp.where((lane >= 16 * y) & (lane < 16 * y + 8), row, tile)
    out_ref[...] = jnp.broadcast_to(tile, out_ref.shape)


def tiles_kernel(tiles_ref, peak_ref, wide_ref):
    ny = lax.axis_size("gy")
    nz = lax.axis_size("gz")
    gy = lax.axis_index("gy")
    gz = lax.axis_index("gz")
    py = lax.rem(gy + ny - 1, ny)
    pz = lax.rem(gz + nz - 1, nz)
    near = lanes((8, 128)) % 16 < 8
    peak_ref[...] = jnp.broadcast_to(jnp.max(tiles_ref[...]), peak_ref.shape)
    for half, row in enumerate((py, gy)):
        low = tiles_ref[row * nz + pz]
        high = tiles_ref[row * nz + gz]
        wide_ref[:, half * 128 : (half + 1) * 128] = jnp.where(near, low, lane_roll(high, 8))


def filter_kernel(wide_ref, below_ref, orbitals_ref, u0_ref, u1_ref, u2_ref, own_ref, w_ref):
    first_half = lanes((8, 128)) % 16 < 8

    def packed(even, odd):
        return jnp.where(first_half, lane_roll(even, -68)[:, :128], lane_roll(odd, -60)[:, :128])

    planes = {}
    for plane in range(3, 13):
        row = below_ref[plane : plane + 1] if plane < 8 else wide_ref[plane - 8 : plane - 7]
        planes[plane] = jnp.broadcast_to(row, (8, 256)) + (3.0 - SHIFT)
        w_ref[plane - 3] = planes[plane]
    for q in range(4):
        own_ref[:, q * 128 : (q + 1) * 128] = packed(planes[4 + 2 * q], planes[5 + 2 * q])

    def around(value):
        return (
            lane_roll(value, 1) + lane_roll(value, -1) + lane_roll(value, 16) + lane_roll(value, -16)
        )

    def filter_rows(step, carry):
        rows = pl.ds(pl.multiple_of(step * 8, 8), 8)
        start = {p: orbitals_ref[rows, p * 256 : (p + 1) * 256] for p in range(2, 14)}
        once = {}
        for p in range(3, 13):
            total = around(start[p]) + (start[p - 1] + start[p + 1])
            once[p] = w_ref[p - 3] * start[p] - 0.5 * total
        twice = {}
        for p in range(4, 12):
            total = around(once[p]) + (once[p - 1] + once[p + 1])
            twice[p] = w_ref[p - 3] * once[p] - 0.5 * total
        for q in range(4):
            at = slice(q * 128, (q + 1) * 128)
            u0_ref[rows, at] = packed(start[4 + 2 * q], start[5 + 2 * q])
            u1_ref[rows, at] = packed(once[4 + 2 * q], once[5 + 2 * q])
            u2_ref[rows, at] = packed(twice[4 + 2 * q], twice[5 + 2 * q])
        return carry

    lax.fori_loop(0, ROWS // 8, filter_rows, 0)


def send_traces(ft, value, sent, held_ref, sems):
    right = split(value)
    half = BODY // 2
    traces = dot3(split(ft[half:]), right)
    at = place()
    copies = []
    for n, flip in enumerate(FLIPS):
        held_ref[n] = traces[n * FLAT : (n + 1) * FLAT]
        copies.append(pltpu.make_async_copy(held_ref.at[n], sent[3].at[at ^ flip], sems.at[n]))
        copies[-1].start()
    traces = dot3(split(ft[:half]), right)
    for slot in range(3):
        sent[slot][...] = traces[slot * FLAT : (slot + 1) * FLAT]
    for copy in copies:
        copy.wait()


def basis_kernel(peaks_ref, u0_ref, u1_ref, u2_ref, vectors_ref,
                 basis_ref, ft_ref, scal_ref, *refs):
    sent, (bt_ref, held_ref, sems) = refs[:-3], refs[-3:]
    top = 6.0 + jnp.max(peaks_ref[...])
    centre = (top + cutoff) / 2.0
    half_width = (top - cutoff) / 2.0
    scal_ref[0] = centre
    scal_ref[1] = half_width
    moved = SHIFT - centre
    start = u0_ref[...]
    square = u2_ref[...] + (2.0 * moved) * u1_ref[...] + (moved * moved) * start
    restricted = square * (2.0 / (half_width * half_width)) - start
    halves = split(restricted)
    intersection = dot3(halves, halves, (((1,), (1,)), ((), ())))
    sigma = jnp.sqrt(jnp.sum(intersection * intersection))
    identity = (
        lax.broadcasted_iota(jnp.int32, (ROWS, ROWS), 0) == lanes((ROWS, ROWS))
    ).astype(jnp.float32)
    current = intersection / sigma
    factor = 1.5 * identity - 0.5 * current
    current = product(current, factor)
    root = factor
    for step in range(NEWTON - 1):
        factor = 1.5 * identity - 0.5 * product(root, current)
        if step < NEWTON - 2:
            current = product(current, factor)
        root = product(factor, root)
    root = root / jnp.sqrt(sigma)
    basis = dot3(split(root), halves)

    basis_ref[...] = basis
    bt_ref[...] = jnp.concatenate([basis, jnp.zeros((128 - ROWS, WIDTH), jnp.float32)], axis=0).T
    lower = (
        jnp.concatenate([bt_ref[yy * 16 : yy * 16 + 8] for yy in range(8)], axis=0),
        jnp.concatenate([bt_ref[q * 128 : q * 128 + 16] for q in range(4)], axis=0),
        bt_ref[pl.ds(0, FLAT, stride=8)],
    )
    upper = (
        jnp.concatenate([bt_ref[392 + yy * 16 : 400 + yy * 16] for yy in range(8)], axis=0),
        jnp.concatenate([bt_ref[q * 128 + 112 : q * 128 + 128] for q in range(4)], axis=0),
        bt_ref[pl.ds(7, FLAT, stride=8)],
    )
    pieces = [
        jnp.where(upper_side(axis, odd), upper[AXES.index(axis)], lower[AXES.index(axis)])
        for axis, odd in SLOTS
    ]
    faces_t = jnp.concatenate(pieces, axis=0)
    ft = faces_t[:, :ROWS]
    ft_ref[...] = ft
    send_traces(ft, vectors_ref[...], sent, held_ref, sems)


def coupling_kernel(basis_ref, own_ref, ft_ref, near_ref, swap_ref):
    basis = basis_ref[...]
    own = own_ref[:1] + SHIFT
    cell = lanes((ROWS, WIDTH))
    z = cell % 8
    y = cell // 16 % 8
    x = cell // 128 * 2 + cell // 8 % 2
    odd = x % 2 == 1

    def gate(ok, value):
        return jnp.where(ok, value, 0.0)

    total = gate(z > 0, lane_roll(basis, 1)) + gate(z < 7, lane_roll(basis, -1))
    total = total + gate(y > 0, lane_roll(basis, 16)) + gate(y < 7, lane_roll(basis, -16))
    total = total + jnp.where(odd, lane_roll(basis, 8), lane_roll(basis, -8))
    total = total + gate(
        (x > 0) & (x < 7), jnp.where(odd, lane_roll(basis, -120), lane_roll(basis, 120))
    )
    applied = own * basis - 0.5 * total
    diagonal = dot3(split(basis), split(applied), (((1,), (1,)), ((), ())))
    half = BODY // 2
    swap_ref[...] = -0.5 * ft_ref[:half].T
    near_ref[:, :half] = -0.5 * ft_ref[half:].T
    near_ref[:, half:] = diagonal


def near_kernel(scal_ref, near_ref, now_ref, cube_ref, out_ref):
    now = now_ref[...]
    at = place()
    stacked = jnp.concatenate([cube_ref[at ^ flip] for flip in FLIPS] + [now], axis=0)
    out_ref[...] = dot3(split(near_ref[...]), split(stacked)) - scal_ref[0] * now


def step_kernel(first, last, scal_ref, swap_ref, ft_ref, part_ref, prior_ref, *refs):
    halos = jnp.concatenate([ref[...] for ref in refs[:3]], axis=0)
    out_ref, rest = refs[3], refs[4:]
    following = (dot3(split(swap_ref[...]), split(halos)) + part_ref[...]) / scal_ref[1]
    if not first:
        following = 2.0 * following - prior_ref[...]
    out_ref[...] = following
    if not last:
        send_traces(ft_ref[...], following, rest[:4], rest[4], rest[5])


def vmem():
    return pl.BlockSpec(memory_space=pltpu.VMEM)


def smem():
    return pl.BlockSpec(memory_space=pltpu.SMEM)


def of(*shape):
    return jax.ShapeDtypeStruct(shape, jnp.float32)


def call(kernel, name, out_shape, in_specs, out_specs, scratch=()):
    return pl.pallas_call(
        kernel,
        out_shape=out_shape,
        in_specs=in_specs,
        out_specs=out_specs,
        scratch_shapes=list(scratch),
        compiler_params=pltpu.CompilerParams(vmem_limit_bytes=GRANT),
        name=name,
    )


def per_device(orbitals, potential, coefficients):
    f32 = jnp.float32
    nx = lax.axis_size("gx")
    plane = lax.axis_size("gy") * lax.axis_size("gz")
    tile = call(tile_kernel, "tile", of(plane, 8, 128), [vmem()], vmem())(potential)
    tiles = lax.all_to_all(tile, ("gy", "gz"), 0, 0)
    peak, wide = call(
        tiles_kernel, "tiles", (of(nx, 1, 128), of(8, 256)), [vmem()], (vmem(), vmem())
    )(tiles)
    peaks = lax.all_to_all(peak, "gx", 0, 0)
    below = shifted(wide, "gx", 1)
    *powers, own = call(
        filter_kernel,
        "powers",
        (of(ROWS, WIDTH),) * 3 + (of(8, WIDTH),),
        [vmem()] * 3,
        (vmem(),) * 4,
        [pltpu.VMEM((10, 8, 256), f32)],
    )(wide, below, orbitals.reshape(ROWS, -1))
    start = coefficients.reshape(ROWS, COLS)
    sent_shapes = (of(FLAT, COLS),) * 3 + (of(CUBE, FLAT, COLS),)
    sent_specs = (vmem(),) * 3 + (pl.BlockSpec(memory_space=pltpu.HBM),)
    staging = [pltpu.VMEM((3, FLAT, COLS), f32), pltpu.SemaphoreType.DMA((3,))]
    basis, ft, scal, *sent = call(
        basis_kernel,
        "basis",
        (of(ROWS, WIDTH), of(BODY, ROWS), of(2)) + sent_shapes,
        [vmem()] * 5,
        (vmem(), vmem(), smem()) + sent_specs,
        [pltpu.VMEM((WIDTH, 128), f32)] + staging,
    )(peaks, *powers, start)
    half = BODY // 2
    near, far = call(
        coupling_kernel, "coupling", (of(ROWS, half + ROWS), of(ROWS, half)), [vmem()] * 3, (vmem(),) * 2
    )(basis, own, ft)

    groups = cubes()
    prior, now = start, start
    for step in range(DG_STEPS):
        halos = [swapped(trace, *pairing) for trace, pairing in zip(sent, SWAPS)]
        cube = lax.all_to_all(sent[3], AXES, 0, 0, axis_index_groups=groups)
        part = call(
            near_kernel, f"near{step}", of(ROWS, COLS), [smem()] + [vmem()] * 3, vmem()
        )(scal, near, now, cube)
        last = step == DG_STEPS - 1

        def body(*refs, step=step, last=last):
            step_kernel(step == 0, last, *refs)

        following, *sent = call(
            body,
            f"step{step}",
            (of(ROWS, COLS),) + (() if last else sent_shapes),
            [smem()] + [vmem()] * 7,
            (vmem(),) + (() if last else sent_specs),
            () if last else staging,
        )(scal, far, ft, part, prior, *halos)
        prior, now = now, following
    return now.reshape(coefficients.shape)


def solution(mesh):
    placed = (P("gx", "gy", "gz", None, None), P("gx", "gy", "gz"), P("gx", "gy", "gz", None, None))
    return jax.shard_map(
        per_device,
        mesh=mesh,
        in_specs=placed,
        out_specs=P("gx", "gy", "gz", None, None),
        check_vma=False,
    )
```

```python
import jax
import jax.numpy as jnp
from jax import lax
from jax.experimental import pallas as pl
from jax.experimental.pallas import tpu as pltpu
from jax.sharding import PartitionSpec as P

NEWTON = 6
DG_STEPS = 3
SHIFT = 3.0
ROWS = 96
EDGE = 8
FLAT = EDGE * EDGE
COLS = 256
FACES = 6
CUBE = 8
GRANT = 16 << 20
BODY = FACES * FLAT
WIDTH = 512
cutoff = 1.0


def shifted(shard, axis, by):
    count = lax.axis_size(axis)
    return lax.ppermute(shard, axis, [(i, (i + by) % count) for i in range(count)])


def split(value):
    high = value.astype(jnp.bfloat16)
    low = (value - high.astype(jnp.float32)).astype(jnp.bfloat16)
    return high, low


def dot3(left, right, dims=(((1,), (0,)), ((), ()))):
    lh, ll = left
    rh, rl = right
    rows = lh.shape[0]

    def one(a, b):
        return lax.dot_general(a, b, dims, preferred_element_type=jnp.float32)

    both = one(jnp.concatenate([lh, ll], axis=0), rh)
    return both[:rows] + (both[rows:] + one(lh, rl))


def exact(left, right, dims=(((1,), (0,)), ((), ()))):
    return lax.dot_general(
        left, right, dims, precision=lax.Precision.HIGHEST, preferred_element_type=jnp.float32
    )


def product(left, right):
    return dot3(split(left), split(right))


def lane_roll(value, by):
    return pltpu.roll(value, by % value.shape[-1], axis=value.ndim - 1)


def lanes(shape):
    return lax.broadcasted_iota(jnp.int32, shape, len(shape) - 1)


SWAPS = (("gx", 1), ("gz", 1), ("gy", 0))
CUBE_PAIRS = (("gx", 0), ("gy", 1), ("gz", 0))
SLOTS = SWAPS + CUBE_PAIRS
AXES = ("gx", "gy", "gz")
FLIPS = (4, 2, 1)


def upper_side(axis, odd):
    return lax.rem(lax.axis_index(axis), 2) == odd


def swapped(shard, axis, odd):
    count = lax.axis_size(axis)
    pairs = [((2 * i + odd) % count, (2 * i + 1 + odd) % count) for i in range(count // 2)]
    return lax.ppermute(shard, axis, pairs + [(b, a) for a, b in pairs])


def place():
    return sum(
        flip * lax.rem(lax.axis_index(axis) + odd, 2) for flip, (axis, odd) in zip(FLIPS, CUBE_PAIRS)
    )


def cubes():
    sizes = [lax.axis_size(axis) for axis in AXES]
    groups = []
    for base in ((i, j, k) for i in range(sizes[0] // 2) for j in range(sizes[1] // 2) for k in range(sizes[2] // 2)):
        group = []
        for spot in range(CUBE):
            x, y, z = [
                (2 * base[n] + CUBE_PAIRS[n][1] + (spot // FLIPS[n]) % 2) % sizes[n] for n in range(3)
            ]
            group.append((x * sizes[1] + y) * sizes[2] + z)
        groups.append(group)
    return groups


def tile_kernel(potential_ref, out_ref):
    lane = lanes((8, 128))
    tile = jnp.full((8, 128), jnp.max(potential_ref[...]))
    for y in range(8):
        row = jnp.concatenate([potential_ref[:, y, :], jnp.zeros((8, 120), jnp.float32)], axis=1)
        if y:
            row = lane_roll(row, 16 * y)
        tile = jnp.where((lane >= 16 * y) & (lane < 16 * y + 8), row, tile)
    out_ref[...] = jnp.broadcast_to(tile, out_ref.shape)


def tiles_kernel(tiles_ref, peak_ref, wide_ref):
    ny = lax.axis_size("gy")
    nz = lax.axis_size("gz")
    gy = lax.axis_index("gy")
    gz = lax.axis_index("gz")
    py = lax.rem(gy + ny - 1, ny)
    pz = lax.rem(gz + nz - 1, nz)
    near = lanes((8, 128)) % 16 < 8
    peak_ref[...] = jnp.broadcast_to(jnp.max(tiles_ref[...]), peak_ref.shape)
    for half, row in enumerate((py, gy)):
        low = tiles_ref[row * nz + pz]
        high = tiles_ref[row * nz + gz]
        wide_ref[:, half * 128 : (half + 1) * 128] = jnp.where(near, low, lane_roll(high, 8))


def filter_kernel(wide_ref, below_ref, orbitals_ref, u0_ref, u1_ref, u2_ref, own_ref, w_ref):
    first_half = lanes((8, 128)) % 16 < 8

    def packed(even, odd):
        return jnp.where(first_half, lane_roll(even, -68)[:, :128], lane_roll(odd, -60)[:, :128])

    planes = {}
    for plane in range(3, 13):
        row = below_ref[plane : plane + 1] if plane < 8 else wide_ref[plane - 8 : plane - 7]
        planes[plane] = jnp.broadcast_to(row, (8, 256)) + (3.0 - SHIFT)
        w_ref[plane - 3] = planes[plane]
    for q in range(4):
        own_ref[:, q * 128 : (q + 1) * 128] = packed(planes[4 + 2 * q], planes[5 + 2 * q])

    def around(value):
        return (
            lane_roll(value, 1) + lane_roll(value, -1) + lane_roll(value, 16) + lane_roll(value, -16)
        )

    def filter_rows(step, carry):
        rows = pl.ds(pl.multiple_of(step * 8, 8), 8)
        start = {p: orbitals_ref[rows, p * 256 : (p + 1) * 256] for p in range(2, 14)}
        once = {}
        for p in range(3, 13):
            total = around(start[p]) + (start[p - 1] + start[p + 1])
            once[p] = w_ref[p - 3] * start[p] - 0.5 * total
        twice = {}
        for p in range(4, 12):
            total = around(once[p]) + (once[p - 1] + once[p + 1])
            twice[p] = w_ref[p - 3] * once[p] - 0.5 * total
        for q in range(4):
            at = slice(q * 128, (q + 1) * 128)
            u0_ref[rows, at] = packed(start[4 + 2 * q], start[5 + 2 * q])
            u1_ref[rows, at] = packed(once[4 + 2 * q], once[5 + 2 * q])
            u2_ref[rows, at] = packed(twice[4 + 2 * q], twice[5 + 2 * q])
        return carry

    lax.fori_loop(0, ROWS // 8, filter_rows, 0)


def send_traces(ft, value, sent, held_ref, sems):
    right = split(value)
    half = BODY // 2
    traces = dot3(split(ft[half:]), right)
    at = place()
    copies = []
    for n, flip in enumerate(FLIPS):
        held_ref[n] = traces[n * FLAT : (n + 1) * FLAT]
        copies.append(pltpu.make_async_copy(held_ref.at[n], sent[3].at[at ^ flip], sems.at[n]))
        copies[-1].start()
    traces = dot3(split(ft[:half]), right)
    for slot in range(3):
        sent[slot][...] = traces[slot * FLAT : (slot + 1) * FLAT]
    for copy in copies:
        copy.wait()


def basis_kernel(peaks_ref, u0_ref, u1_ref, u2_ref, vectors_ref,
                 basis_ref, ft_ref, scal_ref, *refs):
    sent, (bt_ref, held_ref, sems) = refs[:-3], refs[-3:]
    top = 6.0 + jnp.max(peaks_ref[...])
    centre = (top + cutoff) / 2.0
    half_width = (top - cutoff) / 2.0
    scal_ref[0] = centre
    scal_ref[1] = half_width
    moved = SHIFT - centre
    start = u0_ref[...]
    square = u2_ref[...] + (2.0 * moved) * u1_ref[...] + (moved * moved) * start
    restricted = square * (2.0 / (half_width * half_width)) - start
    halves = split(restricted)
    intersection = dot3(halves, halves, (((1,), (1,)), ((), ())))
    sigma = jnp.sqrt(jnp.sum(intersection * intersection))
    identity = (
        lax.broadcasted_iota(jnp.int32, (ROWS, ROWS), 0) == lanes((ROWS, ROWS))
    ).astype(jnp.float32)
    current = intersection / sigma
    factor = 1.5 * identity - 0.5 * current
    current = product(current, factor)
    root = factor
    for step in range(NEWTON - 1):
        factor = 1.5 * identity - 0.5 * product(root, current)
        if step < NEWTON - 2:
            current = product(current, factor)
        root = product(factor, root)
    root = root / jnp.sqrt(sigma)
    basis = dot3(split(root), halves)

    basis_ref[...] = basis
    bt_ref[...] = jnp.concatenate([basis, jnp.zeros((128 - ROWS, WIDTH), jnp.float32)], axis=0).T
    lower = (
        jnp.concatenate([bt_ref[yy * 16 : yy * 16 + 8] for yy in range(8)], axis=0),
        jnp.concatenate([bt_ref[q * 128 : q * 128 + 16] for q in range(4)], axis=0),
        bt_ref[pl.ds(0, FLAT, stride=8)],
    )
    upper = (
        jnp.concatenate([bt_ref[392 + yy * 16 : 400 + yy * 16] for yy in range(8)], axis=0),
        jnp.concatenate([bt_ref[q * 128 + 112 : q * 128 + 128] for q in range(4)], axis=0),
        bt_ref[pl.ds(7, FLAT, stride=8)],
    )
    pieces = [
        jnp.where(upper_side(axis, odd), upper[AXES.index(axis)], lower[AXES.index(axis)])
        for axis, odd in SLOTS
    ]
    faces_t = jnp.concatenate(pieces, axis=0)
    ft = faces_t[:, :ROWS]
    ft_ref[...] = ft
    send_traces(ft, vectors_ref[...], sent, held_ref, sems)


def coupling_kernel(basis_ref, own_ref, ft_ref, near_ref, swap_ref):
    basis = basis_ref[...]
    own = own_ref[:1] + SHIFT
    cell = lanes((ROWS, WIDTH))
    z = cell % 8
    y = cell // 16 % 8
    x = cell // 128 * 2 + cell // 8 % 2
    odd = x % 2 == 1

    def gate(ok, value):
        return jnp.where(ok, value, 0.0)

    total = gate(z > 0, lane_roll(basis, 1)) + gate(z < 7, lane_roll(basis, -1))
    total = total + gate(y > 0, lane_roll(basis, 16)) + gate(y < 7, lane_roll(basis, -16))
    total = total + jnp.where(odd, lane_roll(basis, 8), lane_roll(basis, -8))
    total = total + gate(
        (x > 0) & (x < 7), jnp.where(odd, lane_roll(basis, -120), lane_roll(basis, 120))
    )
    applied = own * basis - 0.5 * total
    diagonal = dot3(split(basis), split(applied), (((1,), (1,)), ((), ())))
    half = BODY // 2
    swap_ref[...] = -0.5 * ft_ref[:half].T
    near_ref[:, :half] = -0.5 * ft_ref[half:].T
    near_ref[:, half:] = diagonal


def near_kernel(scal_ref, near_ref, now_ref, cube_ref, out_ref):
    now = now_ref[...]
    at = place()
    stacked = jnp.concatenate([cube_ref[at ^ flip] for flip in FLIPS] + [now], axis=0)
    out_ref[...] = dot3(split(near_ref[...]), split(stacked)) - scal_ref[0] * now


def step_kernel(first, last, scal_ref, swap_ref, ft_ref, part_ref, prior_ref, *refs):
    halos = jnp.concatenate([ref[...] for ref in refs[:3]], axis=0)
    out_ref, rest = refs[3], refs[4:]
    following = (dot3(split(swap_ref[...]), split(halos)) + part_ref[...]) / scal_ref[1]
    if not first:
        following = 2.0 * following - prior_ref[...]
    out_ref[...] = following
    if not last:
        send_traces(ft_ref[...], following, rest[:4], rest[4], rest[5])


def vmem():
    return pl.BlockSpec(memory_space=pltpu.VMEM)


def smem():
    return pl.BlockSpec(memory_space=pltpu.SMEM)


def of(*shape):
    return jax.ShapeDtypeStruct(shape, jnp.float32)


def call(kernel, name, out_shape, in_specs, out_specs, scratch=()):
    return pl.pallas_call(
        kernel,
        out_shape=out_shape,
        in_specs=in_specs,
        out_specs=out_specs,
        scratch_shapes=list(scratch),
        compiler_params=pltpu.CompilerParams(vmem_limit_bytes=GRANT),
        name=name,
    )


def per_device(orbitals, potential, coefficients):
    f32 = jnp.float32
    nx = lax.axis_size("gx")
    plane = lax.axis_size("gy") * lax.axis_size("gz")
    tile = call(tile_kernel, "tile", of(plane, 8, 128), [vmem()], vmem())(potential)
    tiles = lax.all_to_all(tile, ("gy", "gz"), 0, 0)
    peak, wide = call(
        tiles_kernel, "tiles", (of(nx, 1, 128), of(8, 256)), [vmem()], (vmem(), vmem())
    )(tiles)
    peaks = lax.all_to_all(peak, "gx", 0, 0)
    below = shifted(wide, "gx", 1)
    *powers, own = call(
        filter_kernel,
        "powers",
        (of(ROWS, WIDTH),) * 3 + (of(8, WIDTH),),
        [vmem()] * 3,
        (vmem(),) * 4,
        [pltpu.VMEM((10, 8, 256), f32)],
    )(wide, below, orbitals.reshape(ROWS, -1))
    start = coefficients.reshape(ROWS, COLS)
    sent_shapes = (of(FLAT, COLS),) * 3 + (of(CUBE, FLAT, COLS),)
    sent_specs = (vmem(),) * 3 + (pl.BlockSpec(memory_space=pltpu.HBM),)
    staging = [pltpu.VMEM((3, FLAT, COLS), f32), pltpu.SemaphoreType.DMA((3,))]
    basis, ft, scal, *sent = call(
        basis_kernel,
        "basis",
        (of(ROWS, WIDTH), of(BODY, ROWS), of(2)) + sent_shapes,
        [vmem()] * 5,
        (vmem(), vmem(), smem()) + sent_specs,
        [pltpu.VMEM((WIDTH, 128), f32)] + staging,
    )(peaks, *powers, start)
    half = BODY // 2
    near, far = call(
        coupling_kernel, "coupling", (of(ROWS, half + ROWS), of(ROWS, half)), [vmem()] * 3, (vmem(),) * 2
    )(basis, own, ft)

    groups = cubes()
    prior, now = start, start
    for step in range(DG_STEPS):
        halos = [swapped(trace, *pairing) for trace, pairing in zip(sent, SWAPS)]
        cube = lax.all_to_all(sent[3], AXES, 0, 0, axis_index_groups=groups)
        part = call(
            near_kernel, f"near{step}", of(ROWS, COLS), [smem()] + [vmem()] * 3, vmem()
        )(scal, near, now, cube)
        last = step == DG_STEPS - 1

        def body(*refs, step=step, last=last):
            step_kernel(step == 0, last, *refs)

        following, *sent = call(
            body,
            f"step{step}",
            (of(ROWS, COLS),) + (() if last else sent_shapes),
            [smem()] + [vmem()] * 7,
            (vmem(),) + (() if last else sent_specs),
            () if last else staging,
        )(scal, far, ft, part, prior, *halos)
        prior, now = now, following
    return now.reshape(coefficients.shape)


def solution(mesh):
    placed = (P("gx", "gy", "gz", None, None), P("gx", "gy", "gz"), P("gx", "gy", "gz", None, None))
    return jax.shard_map(
        per_device,
        mesh=mesh,
        in_specs=placed,
        out_specs=P("gx", "gy", "gz", None, None),
        check_vma=False,
    )
```
